128 devices in a mesh: patch: 32 (over y, z, core), band: 4 (over x).
Axes of the slice: x: 4, y: 4, z: 4, core: 2. Of those that a mesh axis runs over, the one named last changes fastest.
Arguments:
- blocks: bfloat16 [4, 1024, 256, 256], P('band', 'patch'), may hold values from -6 to 6
- dest_patch: int32 [4, 1024], P('band', 'patch'), may hold values from 0 to 31, as said below
- dest_slot: int32 [4, 1024], P('band', 'patch'), may hold values from 0 to 3
- weights: bfloat16 [4, 1024], P('band', 'patch'), may hold values from 0.25 to 4
- psf_taps: bfloat16 [4, 1024, 2, 41], P('band', 'patch'), may hold values from -1 to 1
- det_taps: float32 [4, 25], P('band'), may hold values from -1.25 to 1.25
- noise_var: float32 [4], P('band'), may hold values from 0.5 to 2
Outputs:
- coadd_image: float32 [4, 512, 16384], P('band', None, 'patch')
- chi_square: float32 [512, 16384], P('band', 'patch')
The draws below stay inside these ranges and needn't reach their ends.
Inputs may be any that keep to these rules, and one draw needn't show every extreme that they name: `dest_patch`: within each band, among the 32 blocks of one index of patch (aligned runs of 32 blocks), at most 4 go to any one patch; in every band some patch receives exactly 4 blocks from every index of patch.
All inputs are finite; a program needn't handle non-finite values.
Results may differ from the reference program's by a relative error of at most 0.0048.
Values may be sent and summed in bfloat16 or wider, within the bound.
A program may use at most 192 MiB of HBM per device.

```python
import math
import jax
import jax.numpy as jnp
from jax import lax

BLK = 256
TH = 2
TW = 2
VB_DEV = 32
TAPS = 41
DR = 12
CAP = 4
DTAPS = 25
BANDS = 4
VISIT_BLOCKS = 1024
SLOTS = 4
PH = 512
WIDTH = 16384


def draw_dest_patch(key, part):
    npatch = VISIT_BLOCKS // VB_DEV
    key_busy, key_perm, key_order = jax.random.split(jax.random.fold_in(key, 17), 3)
    busiest = jax.random.randint(key_busy, (BANDS, 1, 1), 0, npatch).astype(jnp.int32)
    scores = jax.random.randint(key_perm, (BANDS, npatch, npatch - 1), 0, 1 << 20) * (npatch - 1) + jnp.arange(npatch - 1, dtype=jnp.int32)
    others = jnp.argsort(scores, axis=-1, stable=True).astype(jnp.int32)
    places = jnp.arange(VB_DEV, dtype=jnp.int32)
    picked = jnp.maximum(places - CAP, 0) // CAP
    chosen = jnp.take(others, picked, axis=-1)
    chosen = chosen + (chosen >= busiest).astype(jnp.int32)
    target = jnp.where(places[None, None, :] < CAP, busiest, chosen)
    order_scores = jax.random.randint(key_order, (BANDS, npatch, VB_DEV), 0, 1 << 20) * VB_DEV + places
    ordering = jnp.argsort(order_scores, axis=-1, stable=True)
    target = jnp.take_along_axis(target, ordering, axis=-1)
    return target.reshape(BANDS, VISIT_BLOCKS).astype(jnp.int32)


def touch_ends(drawn, stream_key, low, high):
    longest = drawn.shape.index(max(drawn.shape))
    spots = []
    for shift in (0, 1):
        where = [jax.random.randint(jax.random.fold_in(stream_key, axis), (), 0, length) for axis, length in enumerate(drawn.shape)]
        where[longest] = (where[longest] + shift) % drawn.shape[longest]
        spots.append(tuple(where))
    return drawn.at[spots[0]].set(low).at[spots[1]].set(high)


def levels(rng, shape, cuts, low, top_value):
    factor_of, own = 1.0, jax.random.fold_in(rng, 6)
    for position, parts in cuts:
        draws = jnp.exp(jax.random.uniform(jax.random.fold_in(own, position), (parts,), jnp.float32, low / len(cuts), top_value / len(cuts)))
        factor_of = factor_of * jnp.repeat(draws, shape[position] // parts).reshape([-1 if axis == position else 1 for axis in range(len(shape))])
    return factor_of


def centred(rng, shape, width, most, shards=(), held_as=jnp.bfloat16):
    level = levels(rng, shape, shards, -0.22, 0.18) if shards else 1.0
    result = jax.random.normal(rng, shape, jnp.float32) * width * level
    return jnp.minimum(jnp.maximum(result, -most), most).astype(held_as)


def setup_inputs(seed: int = 0) -> dict:
    key_of = jax.random.split(jax.random.key(seed), 8)
    return {
        "blocks": centred(key_of[0], (BANDS, VISIT_BLOCKS, BLK, BLK), 1.0, 6.0, ((0, 4), (1, 32))),
        "dest_patch": draw_dest_patch(jax.random.fold_in(key_of[7], 71), 0),
        "dest_slot": touch_ends(jax.random.randint(key_of[2], (BANDS, VISIT_BLOCKS), 0, SLOTS), jax.random.fold_in(key_of[2], 1), 0, SLOTS - 1).astype(jnp.int32),
        "weights": jnp.clip(jnp.exp(math.log(4.0) - 2.7725887 * jax.random.uniform(key_of[3], (BANDS, VISIT_BLOCKS), jnp.float32) ** levels(key_of[3], (BANDS, VISIT_BLOCKS), ((0, 4), (1, 32)), -0.2, 0.2)), 0.25, 4.0).astype(jnp.bfloat16),
        "psf_taps": centred(key_of[4], (BANDS, VISIT_BLOCKS, 2, TAPS), TAPS ** -0.5, 1.0, ((0, 4), (1, 32))),
        "det_taps": centred(key_of[5], (BANDS, DTAPS), DTAPS ** -0.5, 1.25, ((0, 4),), jnp.float32),
        "noise_var": jnp.clip(jnp.exp(math.log(2.0) - 1.3862944 * jax.random.uniform(key_of[6], (BANDS,), jnp.float32) ** levels(key_of[6], (BANDS,), ((0, 4),), -0.2, 0.2)), 0.5, 2.0),
    }


def shift_table(kernel, number, extent):
    tap_count = kernel.shape[-1]
    leading = kernel.shape[:-1]
    padded_taps = jnp.concatenate([kernel, jnp.zeros(leading + (extent - tap_count + 1,), kernel.dtype)], axis=-1)
    repeated = jnp.tile(padded_taps, (1,) * len(leading) + (number,))
    return repeated[..., : number * extent].reshape(leading + (number, extent))


def band_rows(kernel, number):
    half_width = kernel.shape[-1] // 2
    table = shift_table(kernel, number, number + 2 * half_width)
    return table[..., :, half_width: half_width + number]


def match_group(grouped):
    group_blocks, group_taps = grouped
    matrices = band_rows(group_taps.astype(jnp.float32), BLK)
    half_pass = jnp.einsum("nij,njk->nik", matrices[:, 0], group_blocks.astype(jnp.float32)).astype(jnp.bfloat16)
    return jnp.einsum("nij,nkj->nik", half_pass.astype(jnp.float32), matrices[:, 1]).astype(jnp.bfloat16)


def reference(blocks, dest_patch, dest_slot, weights, psf_taps, det_taps, noise_var):
    npatch = VISIT_BLOCKS // VB_DEV
    groups = VISIT_BLOCKS // 4
    chi_total = jnp.zeros((PH, WIDTH), jnp.float32)
    images = []
    for band_index in range(BANDS):
        matched = lax.map(match_group, (blocks[band_index].reshape(groups, 4, BLK, BLK), psf_taps[band_index].reshape(groups, 4, 2, TAPS)))
        flattened = matched.reshape(VISIT_BLOCKS, BLK * BLK).astype(jnp.float32)
        target = dest_patch[band_index] * SLOTS + dest_slot[band_index]
        tile_picks = jnp.arange(npatch * SLOTS, dtype=jnp.int32)[:, None] == target[None, :]
        selected = jnp.where(tile_picks, weights[band_index].astype(jnp.float32)[None, :], jnp.zeros((), jnp.float32))
        weighted = jnp.dot(selected, flattened, precision=lax.Precision.HIGHEST)
        weight_sum = jnp.sum(selected, axis=1)
        tile_values = weighted / jnp.maximum(weight_sum, 1.0)[:, None]
        patch_image = tile_values.reshape(npatch, TH, TW, BLK, BLK).transpose(1, 3, 0, 2, 4).reshape(PH, WIDTH)
        images.append(patch_image)
        kernel = det_taps[band_index]
        col_pass = jnp.zeros((PH, WIDTH), jnp.float32)
        for offset in range(DTAPS):
            col_pass = col_pass + kernel[offset] * jnp.roll(patch_image, DR - offset, axis=1)
        padded = jnp.pad(col_pass, ((DR, DR), (0, 0)))
        row_pass = jnp.zeros((PH, WIDTH), jnp.float32)
        for offset in range(DTAPS):
            row_pass = row_pass + kernel[offset] * padded[offset: offset + PH]
        chi_total = chi_total + row_pass * row_pass / noise_var[band_index]
    return jnp.stack(images, axis=0), chi_total
```

```python
import jax
import jax.numpy as jnp
from jax import lax
from jax.experimental import pallas as pl
from jax.experimental.pallas import tpu as pltpu
from jax.sharding import PartitionSpec as P

DR = 12
SLOTS = 4
TAPS = 41
BLK = 256
NPATCH = 32
GROUP = 4


def toeplitz_store(taps_row, matrix):
    rows = jnp.broadcast_to(taps_row, (16, 128))
    skew = pltpu.roll(rows, 0, 1, stride=1, stride_axis=0)
    zeros = jnp.zeros((16, 256), jnp.float32)
    wide = jnp.concatenate([zeros, skew, zeros], axis=1)
    for step in range(-9, 3):
        d = 16 * step
        lo = 256 + d + 20
        tile = wide[:, lo : lo + 128].astype(jnp.bfloat16)
        rb = -step
        if rb >= 0:
            matrix[16 * rb : 16 * rb + 16, 0:128] = tile
        rb = 8 - step
        if rb < 16:
            matrix[16 * rb : 16 * rb + 16, 128:256] = tile


def match_kernel(tile_ref, weight_ref, taps_ref, blocks_hbm, out_ref, bbuf, mats, sems):
    count = bbuf.shape[0]

    def fetch(g):
        return pltpu.make_async_copy(
            blocks_hbm.at[pl.ds(g * GROUP, GROUP)], bbuf.at[pl.ds(g * GROUP, GROUP)], sems.at[g]
        )

    for g in range(count // GROUP):
        fetch(g).start()
    mats[...] = jnp.zeros_like(mats)

    @pl.loop(0, out_ref.shape[0])
    def _(t):
        out_ref[t] = jnp.zeros((BLK, BLK), jnp.bfloat16)

    @pl.loop(0, count // GROUP)
    def _(g):
        fetch(g).wait()
        for n in range(GROUP):
            i = g * GROUP + n
            toeplitz_store(taps_ref[i, 0:1, :], mats.at[n % 2, 0])
            toeplitz_store(taps_ref[i, 1:2, :], mats.at[n % 2, 1])
            half = jnp.dot(
                mats[n % 2, 0], bbuf[i], preferred_element_type=jnp.float32
            ).astype(jnp.bfloat16)
            full = lax.dot_general(
                half, mats[n % 2, 1], (((1,), (1,)), ((), ())), preferred_element_type=jnp.float32
            ).astype(jnp.bfloat16)
            t = tile_ref[i]
            out_ref[t] = (out_ref[t].astype(jnp.float32) + weight_ref[i] * full.astype(jnp.float32)).astype(jnp.bfloat16)


def match_partials(tile, weight, taps, blocks):
    count = blocks.shape[0]
    return pl.pallas_call(
        match_kernel,
        out_shape=jax.ShapeDtypeStruct((NPATCH * SLOTS, BLK, BLK), jnp.bfloat16),
        in_specs=[
            pl.BlockSpec(memory_space=pltpu.SMEM),
            pl.BlockSpec(memory_space=pltpu.SMEM),
            pl.BlockSpec(memory_space=pltpu.VMEM),
            pl.BlockSpec(memory_space=pl.ANY),
        ],
        out_specs=pl.BlockSpec(memory_space=pltpu.VMEM),
        scratch_shapes=[
            pltpu.VMEM((count, BLK, BLK), jnp.bfloat16),
            pltpu.VMEM((2, 2, BLK, BLK), jnp.bfloat16),
            pltpu.SemaphoreType.DMA((count // GROUP,)),
        ],
        compiler_params=pltpu.CompilerParams(vmem_limit_bytes=40 << 20),
        name="match_partials",
    )(tile, weight, taps, blocks)


def split_dot(a, b, dims):
    return lax.dot_general(a, b, dims, precision=lax.Precision.HIGH, preferred_element_type=jnp.float32)


def banded(taps, rows, cols, start):
    offsets = (
        lax.broadcasted_iota(jnp.int32, (rows, cols), 1)
        - lax.broadcasted_iota(jnp.int32, (rows, cols), 0)
        + start
    )
    table = jnp.zeros((rows, cols), jnp.float32)
    for t in range(taps.shape[0]):
        table = table + jnp.where(offsets == t, taps[t], jnp.zeros((), jnp.float32))
    return table


def local(blocks, dest_patch, dest_slot, weights, psf_taps, det_taps, noise_var):
    tile = dest_patch[0] * SLOTS + dest_slot[0]
    weight = weights[0].astype(jnp.float32)
    taps = jnp.pad(psf_taps[0].astype(jnp.float32), ((0, 0), (0, 0), (0, 128 - TAPS)))
    hits = jnp.where(tile[:, None] == jnp.arange(NPATCH * SLOTS, dtype=jnp.int32)[None, :], weight[:, None], 0.0)
    weight_part = jnp.sum(hits, axis=0).reshape(NPATCH, SLOTS)
    weight_sum = lax.psum_scatter(weight_part, "patch", scatter_dimension=0, tiled=True)[0]
    partial = match_partials(tile, weight, taps, blocks[0])
    total = lax.psum_scatter(partial, "patch", scatter_dimension=0, tiled=True)
    values = total.astype(jnp.float32) / jnp.maximum(weight_sum, 1.0)[:, None, None]
    image = values.reshape(2, 2, BLK, BLK).transpose(0, 2, 1, 3).reshape(2 * BLK, 2 * BLK)
    size = NPATCH
    up = [(i, (i + 1) % size) for i in range(size)]
    down = [(j, i) for i, j in up]
    before = lax.ppermute(image[:, -DR:], "patch", up)
    after = lax.ppermute(image[:, :DR], "patch", down)
    padded = jnp.concatenate([before, image, after], axis=1)
    kernel = det_taps[0]
    col_table = banded(kernel, 2 * BLK, 2 * BLK + 2 * DR, 0)
    row_table = banded(kernel, 2 * BLK, 2 * BLK, DR)
    col_pass = split_dot(padded, col_table, (((1,), (1,)), ((), ())))
    row_pass = split_dot(row_table, col_pass, (((1,), (0,)), ((), ())))
    term = row_pass * row_pass / noise_var[0]
    chi = lax.psum_scatter(term, "band", scatter_dimension=0, tiled=True)
    return image[None], chi


def solution(mesh):
    in_specs = (
        P("band", "patch", None, None),
        P("band", "patch"),
        P("band", "patch"),
        P("band", "patch"),
        P("band", "patch", None, None),
        P("band", None),
        P("band"),
    )
    out_specs = (P("band", None, "patch"), P("band", "patch"))
    return jax.shard_map(local, mesh=mesh, in_specs=in_specs, out_specs=out_specs, check_vma=False)
```

```python
import jax
import jax.numpy as jnp
from jax import lax
from jax.experimental import pallas as pl
from jax.experimental.pallas import tpu as pltpu
from jax.sharding import PartitionSpec as P

DR = 12
DTAPS = 25
SLOTS = 4
TAPS = 41
BLK = 256
PH = 512
NPATCH = 32
NBAND = 4
SIDE = 4
GROUP = 4
STREAMS = ((1, 1), (1, -1), (0, 1), (0, -1))
BF16 = jnp.bfloat16
F32 = jnp.float32


def toeplitz_store(taps_row, matrix):
    rows = jnp.broadcast_to(taps_row, (16, 128))
    skew = pltpu.roll(rows, 0, 1, stride=1, stride_axis=0)
    zeros = jnp.zeros((16, 256), F32)
    wide = jnp.concatenate([zeros, skew, zeros], axis=1)
    for step in range(-9, 3):
        lo = 256 + 16 * step + 20
        tile = wide[:, lo : lo + 128].astype(BF16)
        rb = -step
        if rb >= 0:
            matrix[16 * rb : 16 * rb + 16, 0:128] = tile
        rb = 8 - step
        if rb < 16:
            matrix[16 * rb : 16 * rb + 16, 128:256] = tile


def match_kernel(tile_ref, weight_ref, taps_ref, blocks_ref, out_ref, mats):
    count = blocks_ref.shape[0]
    mats[...] = jnp.zeros_like(mats)

    @pl.loop(0, out_ref.shape[0])
    def _(t):
        out_ref[t] = jnp.zeros((BLK, BLK), BF16)

    @pl.loop(0, count // GROUP)
    def _(g):
        for n in range(GROUP):
            for axis in range(2):
                toeplitz_store(taps_ref[g * GROUP + n, axis : axis + 1, :], mats.at[n, axis])
        halves = []
        for n in range(GROUP):
            half = jnp.dot(mats[n, 0], blocks_ref[g * GROUP + n], preferred_element_type=F32)
            halves.append(half.astype(BF16))
        for n in range(GROUP):
            i = g * GROUP + n
            full = jnp.dot(halves[n], mats[n, 1], preferred_element_type=F32).astype(BF16)
            t = tile_ref[i]
            out_ref[t] = (out_ref[t].astype(F32) + weight_ref[i] * full.astype(F32)).astype(BF16)


def match_partials(tile, weight, taps, blocks):
    smem = pl.BlockSpec(memory_space=pltpu.SMEM)
    vmem = pl.BlockSpec(memory_space=pltpu.VMEM)
    return pl.pallas_call(
        match_kernel,
        out_shape=pltpu.VMEM((NPATCH * SLOTS, BLK, BLK), BF16),
        in_specs=[smem, smem, vmem, vmem],
        out_specs=vmem,
        scratch_shapes=[pltpu.VMEM((GROUP, 2, BLK, BLK), BF16)],
        compiler_params=pltpu.CompilerParams(vmem_limit_bytes=40 << 20),
        name="match_partials",
    )(tile, weight, taps, blocks)


def wrap(x):
    return lax.rem(x + 2 * SIDE, SIDE)


def patch_index(y, z, core):
    return (y * SIDE + z) * 2 + core


def split(x):
    high = x.astype(BF16)
    return high, (x - high.astype(F32)).astype(BF16)


def dot3(ah, al, bh, bl):
    dot = lambda a, b: jnp.dot(a, b, preferred_element_type=F32)
    return dot(ah, bh) + (dot(ah, bl) + dot(al, bh))


def tap_block(det_ref, shift, sign):
    offset = lax.broadcasted_iota(jnp.int32, (128, 128), 1) - lax.broadcasted_iota(jnp.int32, (128, 128), 0)
    offset = sign * offset + shift + DR
    block = jnp.zeros((128, 128), F32)
    for t in range(DTAPS):
        block = jnp.where(offset == t, det_ref[t], block)
    return block


def build_tables(det_ref, col_tab, row_tab):
    col_tab[...] = jnp.zeros_like(col_tab)
    row_tab[...] = jnp.zeros_like(row_tab)
    for table, sign in ((row_tab, 1), (col_tab, -1)):
        for diag in (-1, 0, 1):
            high, low = split(tap_block(det_ref, sign * 128 * diag, sign))
            for rb in range(PH // 128):
                cb = rb + diag
                if 0 <= cb < PH // 128:
                    table[0, 128 * rb : 128 * rb + 128, 128 * cb : 128 * cb + 128] = high
                    table[1, 128 * rb : 128 * rb + 128, 128 * cb : 128 * cb + 128] = low


def reduce_kernel(
    d_ref, w_ref, det_ref, noise_ref, img_ref, chi_ref,
    pair, hop1, hop2, w_in, halo_out, halo_in, col_tab, row_tab, high, low, term_own, term_out, term_in,
    pair_sem, hop1_sem, hop2_sem, send_sem, w_sem, halo_sem, term_sem,
):
    me = lax.axis_index("patch")
    band = lax.axis_index("band")
    core = lax.rem(me, 2)
    place = (lax.div(me, 2 * SIDE), lax.rem(lax.div(me, 2), SIDE))
    partner = me + 1 - 2 * core

    barrier = pltpu.get_barrier_semaphore()

    def greet(axis, device):
        pl.semaphore_signal(barrier, inc=1, device_id={axis: device})

    @pl.loop(1, NPATCH)
    def _(k):
        greet("patch", lax.rem(me + k, NPATCH))

    for k in range(1, NBAND):
        greet("band", lax.rem(band + k, NBAND))
    pl.semaphore_wait(barrier, NPATCH - 1 + NBAND - 1)

    def remote(src, dst, send, recv, device, axis="patch"):
        return pltpu.make_async_remote_copy(
            src_ref=src, dst_ref=dst, send_sem=send, recv_sem=recv, device_id={axis: device}
        )

    def dest(s, h, k, parity):
        axis, step = STREAMS[s]
        first = wrap(place[axis] - step * (1 + h))
        other = wrap(place[1 - axis] - step * (1 + k))
        y, z = (first, other) if axis == 0 else (other, first)
        return patch_index(y, z, parity) * SLOTS + s

    def neighbour(s, stage):
        axis, step = STREAMS[s]
        axis = axis if stage == 1 else 1 - axis
        moved = list(place)
        moved[axis] = wrap(place[axis] + step)
        return patch_index(moved[0], moved[1], core)

    next1 = [neighbour(s, 1) for s in range(SLOTS)]
    next2 = [neighbour(s, 2) for s in range(SLOTS)]

    def send_pair(s, h, k):
        remote(
            d_ref.at[dest(s, h, k, 1 - core)], pair.at[s, h, k], send_sem.at[0], pair_sem.at[s, h, k], partner
        ).start()

    def wait_pair(s, h, k):
        remote(pair.at[s, h, k], pair.at[s, h, k], send_sem.at[0], pair_sem.at[s, h, k], partner).wait_recv()

    def hop1_copy(s, h, k):
        return remote(pair.at[s, h, k], hop1.at[s, h, k], send_sem.at[1], hop1_sem.at[s, h, k], next1[s])

    def hop2_copy(s, k):
        return remote(pair.at[s, 3, k], hop2.at[s, k], send_sem.at[2], hop2_sem.at[s, k], next2[s])

    @pl.loop(0, SIDE)
    def _(k):
        for s in range(SLOTS):
            send_pair(s, 0, k)

    @pl.loop(1, NPATCH)
    def _(k):
        device = lax.rem(me + k, NPATCH)
        remote(w_ref.at[device], w_in.at[k - 1], send_sem.at[3], w_sem.at[0], device).start()

    def here(s, h, k):
        return d_ref[dest(s, h, k, core)].astype(F32) + pair[s, h, k].astype(F32)

    @pl.loop(0, SIDE)
    def _(k):
        for s in range(SLOTS):
            wait_pair(s, 0, k)
            pair[s, 0, k] = here(s, 0, k).astype(BF16)
            hop1_copy(s, 0, k).start()
            send_pair(s, 1, k)

    build_tables(det_ref, col_tab, row_tab)

    @pl.loop(1, SIDE - 1)
    def _(h):
        @pl.loop(0, SIDE)
        def _(k):
            for s in range(SLOTS):
                send_pair(s, h + 1, k)
            for s in range(SLOTS):
                wait_pair(s, h, k)
                hop1_copy(s, h - 1, k).wait_recv()
                pair[s, h, k] = (here(s, h, k) + hop1[s, h - 1, k].astype(F32)).astype(BF16)
                hop1_copy(s, h, k).start()

    def gathered(s, k):
        wait_pair(s, 3, k)
        hop1_copy(s, 2, k).wait_recv()
        return here(s, 3, k) + hop1[s, 2, k].astype(F32)

    for s in range(SLOTS):
        pair[s, 3, 0] = gathered(s, 0).astype(BF16)
        hop2_copy(s, 0).start()

    @pl.loop(1, SIDE - 1)
    def _(k):
        for s in range(SLOTS):
            total = gathered(s, k)
            hop2_copy(s, k - 1).wait_recv()
            pair[s, 3, k] = (total + hop2[s, k - 1].astype(F32)).astype(BF16)
            hop2_copy(s, k).start()

    all_w = remote(w_in, w_in, send_sem.at[3], w_sem.at[0], partner)
    all_w.wait_recv()
    weight_sum = w_ref[me]
    for k in range(NPATCH - 1):
        weight_sum = weight_sum + w_in[k]
    scale = jnp.maximum(weight_sum, 1.0)

    for s in range(SLOTS):
        total = gathered(s, 3)
        hop2_copy(s, 2).wait_recv()
        total = total + hop2[s, 2].astype(F32)
        divisor = jnp.broadcast_to(scale[s : s + 1, 0:1], (BLK, BLK))
        value = total / divisor
        rows = slice((s // 2) * BLK, (s // 2 + 1) * BLK)
        cols = slice((s % 2) * BLK, (s % 2 + 1) * BLK)
        img_ref[rows, cols] = value
        high[rows, cols], low[rows, cols] = split(value)

    halo_out[0] = high[:, 0:128]
    halo_out[1] = high[:, PH - 128 : PH]
    before = lax.rem(me + NPATCH - 1, NPATCH)
    after = lax.rem(me + 1, NPATCH)
    to_before = remote(halo_out.at[0], halo_in.at[1], send_sem.at[4], halo_sem.at[1], before)
    to_after = remote(halo_out.at[1], halo_in.at[0], send_sem.at[5], halo_sem.at[0], after)
    to_before.start()
    to_after.start()
    col = dot3(high[...], low[...], col_tab[0], col_tab[1])
    to_before.wait_recv()
    to_after.wait_recv()
    dot = lambda a, b: jnp.dot(a, b, preferred_element_type=F32)
    left = halo_in[0]
    right = halo_in[1]
    from_left = dot(left, col_tab[0, 0:128, 128:256]) + dot(left, col_tab[1, 0:128, 128:256])
    from_right = dot(right, col_tab[0, 128:256, 0:128]) + dot(right, col_tab[1, 128:256, 0:128])
    col = jnp.concatenate(
        [col[:, 0:128] + from_left, col[:, 128 : PH - 128], col[:, PH - 128 : PH] + from_right], axis=1
    )
    high[...], low[...] = split(col)
    row = dot3(row_tab[0], row_tab[1], high[...], low[...])
    term = row * row / noise_ref[0]
    height = PH // NBAND
    for g in range(NBAND):
        part = term[g * height : (g + 1) * height]
        term_own[g] = part
        term_out[g] = part.astype(BF16)

    def term_copy(k):
        target = lax.rem(band + k, NBAND)
        return remote(
            term_out.at[target], term_in.at[k - 1], send_sem.at[5 + k], term_sem.at[k - 1], target, "band"
        )

    for k in range(1, NBAND):
        term_copy(k).start()
    chi = term_own[band]
    for k in range(1, NBAND):
        term_copy(k).wait_recv()
        chi = chi + term_in[k - 1].astype(F32)
    chi_ref[...] = chi

    for index, ref in enumerate((pair, hop1, hop2, w_in)):
        remote(ref, ref, send_sem.at[index], w_sem.at[0], partner).wait_send()
    to_before.wait_send()
    to_after.wait_send()
    for k in range(1, NBAND):
        term_copy(k).wait_send()


def reduce_partials(partial, weight_table, det_taps, noise_var):
    smem = pl.BlockSpec(memory_space=pltpu.SMEM)
    vmem = pl.BlockSpec(memory_space=pltpu.VMEM)
    dma = pltpu.SemaphoreType.DMA
    height = PH // NBAND
    return pl.pallas_call(
        reduce_kernel,
        out_shape=(
            jax.ShapeDtypeStruct((PH, PH), F32),
            jax.ShapeDtypeStruct((height, PH), F32),
        ),
        in_specs=[vmem, vmem, smem, smem],
        out_specs=(vmem, vmem),
        scratch_shapes=[
            pltpu.VMEM((SLOTS, SIDE, SIDE, BLK, BLK), BF16),
            pltpu.VMEM((SLOTS, SIDE - 1, SIDE, BLK, BLK), BF16),
            pltpu.VMEM((SLOTS, SIDE - 1, BLK, BLK), BF16),
            pltpu.VMEM((NPATCH - 1, 8, 128), F32),
            pltpu.VMEM((2, PH, 128), BF16),
            pltpu.VMEM((2, PH, 128), BF16),
            pltpu.VMEM((2, PH, PH), BF16),
            pltpu.VMEM((2, PH, PH), BF16),
            pltpu.VMEM((PH, PH), BF16),
            pltpu.VMEM((PH, PH), BF16),
            pltpu.VMEM((NBAND, height, PH), F32),
            pltpu.VMEM((NBAND, height, PH), BF16),
            pltpu.VMEM((NBAND - 1, height, PH), BF16),
            dma((SLOTS, SIDE, SIDE)),
            dma((SLOTS, SIDE - 1, SIDE)),
            dma((SLOTS, SIDE - 1)),
            dma((9,)),
            dma((1,)),
            dma((2,)),
            dma((NBAND - 1,)),
        ],
        compiler_params=pltpu.CompilerParams(
            vmem_limit_bytes=48 << 20, collective_id=0, has_side_effects=True
        ),
        name="reduce_partials",
    )(partial, weight_table, det_taps, noise_var)


def local(blocks, dest_patch, dest_slot, weights, psf_taps, det_taps, noise_var):
    tile = dest_patch[0] * SLOTS + dest_slot[0]
    weight = weights[0].astype(F32)
    taps = psf_taps[0].astype(F32)
    taps = jnp.stack([taps[:, 0], taps[:, 1, ::-1]], axis=1)
    taps = jnp.pad(taps, ((0, 0), (0, 0), (0, 128 - TAPS)))
    slots = jnp.arange(NPATCH * 8, dtype=jnp.int32)
    slots = jnp.where(slots % 8 < SLOTS, slots // 8 * SLOTS + slots % 8, -1)
    hits = jnp.where(tile[:, None] == slots[None, :], weight[:, None], 0.0)
    weight_table = jnp.broadcast_to(jnp.sum(hits, axis=0).reshape(NPATCH, 8, 1), (NPATCH, 8, 128))
    partial = match_partials(tile, weight, taps, blocks[0])
    image, chi = reduce_partials(partial, weight_table, det_taps[0], noise_var)
    return image[None], chi


def solution(mesh):
    in_specs = (
        P("band", "patch", None, None),
        P("band", "patch"),
        P("band", "patch"),
        P("band", "patch"),
        P("band", "patch", None, None),
        P("band", None),
        P("band"),
    )
    out_specs = (P("band", None, "patch"), P("band", "patch"))
    return jax.shard_map(local, mesh=mesh, in_specs=in_specs, out_specs=out_specs, check_vma=False)
```

```python
import jax
import jax.numpy as jnp
from jax import lax
from jax.experimental import pallas as pl
from jax.experimental.pallas import tpu as pltpu
from jax.sharding import PartitionSpec as P

DR = 12
DTAPS = 25
SLOTS = 4
TAPS = 41
BLK = 256
PH = 512
NPATCH = 32
NBAND = 4
SIDE = 4
GROUP = 4
STREAMS = ((1, 1), (1, -1), (0, 1), (0, -1))
BF16 = jnp.bfloat16
F32 = jnp.float32


def toeplitz_store(taps_row, matrix):
    rows = jnp.broadcast_to(taps_row, (16, 128))
    skew = pltpu.roll(rows, 0, 1, stride=1, stride_axis=0)
    zeros = jnp.zeros((16, 256), F32)
    wide = jnp.concatenate([zeros, skew, zeros], axis=1)
    for step in range(-9, 3):
        lo = 256 + 16 * step + 20
        tile = wide[:, lo : lo + 128].astype(BF16)
        rb = -step
        if rb >= 0:
            matrix[16 * rb : 16 * rb + 16, 0:128] = tile
        rb = 8 - step
        if rb < 16:
            matrix[16 * rb : 16 * rb + 16, 128:256] = tile


def match_kernel(
    patch_hbm, slot_hbm, weight_hbm, taps_ref, blocks_hbm, out_ref,
    patch_ref, slot_ref, weight_ref, blocks, table_ref, tap_rows, weight_rows, mats, sems, small_sems,
):
    count = blocks.shape[0]

    def fetch(g):
        part = pl.ds(g * GROUP, GROUP)
        return pltpu.make_async_copy(blocks_hbm.at[0, part], blocks.at[part], sems.at[g])

    small = [
        pltpu.make_async_copy(src, dst, small_sems.at[n])
        for n, (src, dst) in enumerate(((weight_hbm, weight_ref), (patch_hbm, patch_ref), (slot_hbm, slot_ref)))
    ]
    for copy in small:
        copy.start()
    for g in range(count // GROUP):
        fetch(g).start()
    mats[...] = jnp.zeros_like(mats)
    table_ref[...] = jnp.zeros_like(table_ref)
    tap_rows[0] = taps_ref[0].astype(F32)
    ends = lax.broadcasted_iota(jnp.int32, (128, 128), 0) + lax.broadcasted_iota(jnp.int32, (128, 128), 1)
    reverse = jnp.where(ends == TAPS - 1, 1.0, 0.0).astype(BF16)
    tap_rows[1] = jnp.dot(taps_ref[1], reverse, preferred_element_type=F32)
    for copy in small:
        copy.wait()
    diagonal = lax.broadcasted_iota(jnp.int32, (count, count), 0) == lax.broadcasted_iota(jnp.int32, (count, count), 1)
    spread = jnp.where(diagonal, jnp.broadcast_to(weight_ref[...].astype(F32), (count, count)), 0.0)
    weight_rows[...] = jnp.broadcast_to(jnp.sum(spread, axis=1, keepdims=True), (count, 128))

    @pl.loop(0, count // GROUP)
    def _(g):
        fetch(g).wait()
        for n in range(GROUP):
            for axis in range(2):
                toeplitz_store(tap_rows[axis, pl.ds(g * GROUP + n, 1), :], mats.at[n, axis])
        halves = []
        for n in range(GROUP):
            half = jnp.dot(mats[n, 0], blocks[g * GROUP + n], preferred_element_type=F32)
            halves.append(half.astype(BF16))
        for n in range(GROUP):
            i = g * GROUP + n
            full = jnp.dot(halves[n], mats[n, 1], preferred_element_type=F32).astype(BF16)
            weight = weight_rows[pl.ds(i, 1), :]
            patch = patch_ref[0, i]
            slot = slot_ref[0, i]
            place = (patch & 1) * (SIDE * SIDE) + ((patch >> 1) & (SIDE - 1)) * SIDE + (patch >> 3)
            before = table_ref[place, pl.ds(slot, 1), :]
            table_ref[place, pl.ds(slot, 1), :] = before + weight
            wide = lambda row: jnp.broadcast_to(jnp.concatenate([row, row], axis=1), (BLK, BLK))
            tile = patch * SLOTS + slot
            old = jnp.where(wide(before) > 0.0, out_ref[tile].astype(F32), 0.0)
            out_ref[tile] = (old + wide(weight) * full.astype(F32)).astype(BF16)

    high, low = split(table_ref[...].reshape(NPATCH * 8, 128))
    out_ref[NPATCH * SLOTS, :, 0:128] = high
    out_ref[NPATCH * SLOTS, :, 128:256] = low


def match_partials(blocks, dest_patch, dest_slot, weights, taps):
    count = blocks.shape[1]
    hbm = pl.BlockSpec(memory_space=pltpu.HBM)
    vmem = pl.BlockSpec(memory_space=pltpu.VMEM)
    keep = lambda x: pltpu.with_memory_space_constraint(x, pltpu.HBM)
    return pl.pallas_call(
        match_kernel,
        out_shape=pltpu.VMEM((NPATCH * SLOTS + 1, BLK, BLK), BF16),
        in_specs=[hbm, hbm, hbm, vmem, hbm],
        out_specs=vmem,
        scratch_shapes=[
            pltpu.SMEM((1, count), jnp.int32),
            pltpu.SMEM((1, count), jnp.int32),
            pltpu.VMEM((1, count), BF16),
            pltpu.VMEM((count, BLK, BLK), BF16),
            pltpu.VMEM((NPATCH, 8, 128), F32),
            pltpu.VMEM((2, count, 128), F32),
            pltpu.VMEM((count, 128), F32),
            pltpu.VMEM((GROUP, 2, BLK, BLK), BF16),
            pltpu.SemaphoreType.DMA((count // GROUP,)),
            pltpu.SemaphoreType.DMA((3,)),
        ],
        compiler_params=pltpu.CompilerParams(vmem_limit_bytes=28 << 20),
        name="match_partials",
    )(keep(dest_patch), keep(dest_slot), keep(weights), taps, keep(blocks))


def wrap(x):
    return lax.rem(x + 2 * SIDE, SIDE)


def patch_index(y, z, core):
    return (y * SIDE + z) * 2 + core


def split(x):
    high = x.astype(BF16)
    return high, (x - high.astype(F32)).astype(BF16)


def dot3(ah, al, bh, bl):
    dot = lambda a, b: jnp.dot(a, b, preferred_element_type=F32)
    return dot(ah, bh) + (dot(ah, bl) + dot(al, bh))


def tap_block(det_ref, shift, sign):
    offset = lax.broadcasted_iota(jnp.int32, (128, 128), 1) - lax.broadcasted_iota(jnp.int32, (128, 128), 0)
    offset = sign * offset + shift + DR
    block = jnp.zeros((128, 128), F32)
    for t in range(DTAPS):
        block = jnp.where(offset == t, det_ref[t], block)
    return block


def build_tables(det_ref, col_tab, row_tab):
    col_tab[...] = jnp.zeros_like(col_tab)
    row_tab[...] = jnp.zeros_like(row_tab)
    for table, sign in ((row_tab, 1), (col_tab, -1)):
        for diag in (-1, 0, 1):
            high, low = split(tap_block(det_ref, sign * 128 * diag, sign))
            for rb in range(PH // 128):
                cb = rb + diag
                if 0 <= cb < PH // 128:
                    table[0, 128 * rb : 128 * rb + 128, 128 * cb : 128 * cb + 128] = high
                    table[1, 128 * rb : 128 * rb + 128, 128 * cb : 128 * cb + 128] = low


def reduce_kernel(
    d_ref, det_ref, noise_ref, img_ref, chi_ref,
    pair, hop1, hop2, w_ref, w_pair, w_acc, w_hop1, w_hop2, halo_out, halo_in, col_tab, row_tab, high, low,
    term, far_out, far_in, near_out, near_in,
    pair_sem, hop1_sem, hop2_sem, send_sem, w_sem, halo_sem, far_sem, near_sem, end_sem,
):
    me = lax.axis_index("patch")
    band = lax.axis_index("band")
    core = lax.rem(me, 2)
    place = (lax.div(me, 2 * SIDE), lax.rem(lax.div(me, 2), SIDE))
    partner = me + 1 - 2 * core
    before = lax.rem(me + NPATCH - 1, NPATCH)
    after = lax.rem(me + 1, NPATCH)
    beside = lax.rem(me + NPATCH - 1 + 2 * core, NPATCH)

    def moved(axis, step):
        there = list(place)
        there[axis] = wrap(place[axis] + step)
        return patch_index(there[0], there[1], core)

    barrier = pltpu.get_barrier_semaphore()
    for device in (partner, beside, moved(0, 1), moved(0, -1), moved(1, 1), moved(1, -1)):
        pl.semaphore_signal(barrier, inc=1, device_id={"patch": device})
    above = lax.rem(band + 1, NBAND)
    below = lax.rem(band + NBAND - 1, NBAND)
    for device in (above, below):
        pl.semaphore_signal(barrier, inc=1, device_id={"band": device})
    pl.semaphore_wait(barrier, 8)

    def remote(src, dst, send, recv, device, axis="patch"):
        return pltpu.make_async_remote_copy(
            src_ref=src, dst_ref=dst, send_sem=send, recv_sem=recv, device_id={axis: device}
        )

    def dest(s, h, k):
        axis, step = STREAMS[s]
        first = wrap(place[axis] - step * (1 + h))
        other = wrap(place[1 - axis] - step * (1 + k))
        return (first, other) if axis == 0 else (other, first)

    def tile(s, h, k, parity):
        y, z = dest(s, h, k)
        return patch_index(y, z, parity) * SLOTS + s

    next1 = [moved(axis, step) for axis, step in STREAMS]
    next2 = [moved(1 - axis, step) for axis, step in STREAMS]

    def send_pair(s, h, k):
        remote(
            d_ref.at[tile(s, h, k, 1 - core)], pair.at[s, h, k], send_sem.at[0], pair_sem.at[s, h, k], partner
        ).start()

    def wait_pair(s, h, k):
        remote(pair.at[s, h, k], pair.at[s, h, k], send_sem.at[0], pair_sem.at[s, h, k], partner).wait_recv()

    def hop1_copy(s, h, k):
        return remote(pair.at[s, h, k], hop1.at[s, h, k], send_sem.at[1], hop1_sem.at[s, h, k], next1[s])

    def hop2_copy(s, k):
        return remote(pair.at[s, 3, k], hop2.at[s, k], send_sem.at[2], hop2_sem.at[s, k], next2[s])

    table = d_ref[NPATCH * SLOTS]
    table = table[:, 0:128].astype(F32) + table[:, 128:256].astype(F32)
    w_ref[...] = table.reshape(2, SIDE, SIDE, 8, 128)
    w_exchange = remote(w_ref.at[1 - core], w_pair, send_sem.at[3], w_sem.at[0], partner)
    w_exchange.start()

    @pl.loop(0, SIDE)
    def _(k):
        for s in range(SLOTS):
            send_pair(s, 0, k)

    w_exchange.wait_recv()

    def w_here(h):
        z = wrap(place[1] - 1 - h)
        return w_ref[core, z] + w_pair[z]

    def w_copy1(h):
        return remote(w_acc.at[h], w_hop1.at[h], send_sem.at[4 + h], w_sem.at[1 + h], moved(1, 1))

    def w_copy2(k):
        return remote(w_acc.at[3 + k], w_hop2.at[k], send_sem.at[7 + k], w_sem.at[4 + k], moved(0, 1))

    def here(s, h, k):
        y, z = dest(s, h, k)
        wide = lambda row: jnp.broadcast_to(jnp.concatenate([row, row], axis=1), (BLK, BLK))
        mine = jnp.where(
            wide(w_ref[core, z, y, s : s + 1]) > 0.0, d_ref[tile(s, h, k, core)].astype(F32), 0.0
        )
        other = jnp.where(wide(w_pair[z, y, s : s + 1]) > 0.0, pair[s, h, k].astype(F32), 0.0)
        return mine + other

    w_acc[0] = w_here(0)
    w_copy1(0).start()

    @pl.loop(0, SIDE)
    def _(k):
        for s in range(SLOTS):
            wait_pair(s, 0, k)
            pair[s, 0, k] = here(s, 0, k).astype(BF16)
            hop1_copy(s, 0, k).start()
            send_pair(s, 1, k)

    build_tables(det_ref, col_tab, row_tab)

    @pl.loop(1, SIDE - 1)
    def _(h):
        @pl.loop(0, SIDE)
        def _(k):
            for s in range(SLOTS):
                send_pair(s, h + 1, k)
            for s in range(SLOTS):
                wait_pair(s, h, k)
                total = here(s, h, k)
                hop1_copy(s, h - 1, k).wait_recv()
                pair[s, h, k] = (total + hop1[s, h - 1, k].astype(F32)).astype(BF16)
                hop1_copy(s, h, k).start()

        w_copy1(h - 1).wait_recv()
        w_acc[h] = w_here(h) + w_hop1[h - 1]
        w_copy1(h).start()

    def gathered(s, k):
        wait_pair(s, 3, k)
        hop1_copy(s, 2, k).wait_recv()
        return here(s, 3, k) + hop1[s, 2, k].astype(F32)

    for s in range(SLOTS):
        pair[s, 3, 0] = gathered(s, 0).astype(BF16)
        hop2_copy(s, 0).start()

    w_copy1(2).wait_recv()
    w_acc[3] = w_here(3) + w_hop1[2]
    w_copy2(0).start()

    @pl.loop(1, SIDE - 1)
    def _(k):
        for s in range(SLOTS):
            total = gathered(s, k)
            hop2_copy(s, k - 1).wait_recv()
            pair[s, 3, k] = (total + hop2[s, k - 1].astype(F32)).astype(BF16)
            hop2_copy(s, k).start()
        w_copy2(k - 1).wait_recv()
        w_acc[3 + k] = w_acc[3] + w_hop2[k - 1]
        w_copy2(k).start()

    w_copy2(2).wait_recv()
    weight_sum = w_acc[3, place[0]] + w_hop2[2, place[0]]
    scale = jnp.maximum(weight_sum, 1.0)

    for s in range(SLOTS):
        total = gathered(s, 3)
        hop2_copy(s, 2).wait_recv()
        total = total + hop2[s, 2].astype(F32)
        divisor = jnp.broadcast_to(scale[s : s + 1, 0:1], (BLK, BLK))
        value = total / divisor
        rows = slice((s // 2) * BLK, (s // 2 + 1) * BLK)
        cols = slice((s % 2) * BLK, (s % 2 + 1) * BLK)
        img_ref[rows, cols] = value
        high[rows, cols], low[rows, cols] = split(value)

    halo_out[0] = high[:, 0:128]
    halo_out[1] = high[:, PH - 128 : PH]
    to_before = remote(halo_out.at[0], halo_in.at[1], end_sem.at[0], halo_sem.at[1], before)
    to_after = remote(halo_out.at[1], halo_in.at[0], end_sem.at[1], halo_sem.at[0], after)
    to_before.start()
    to_after.start()
    high[...], low[...] = split(dot3(high[...], low[...], col_tab[0], col_tab[1]))
    row = dot3(row_tab[0], row_tab[1], high[...], low[...])
    to_before.wait_recv()
    to_after.wait_recv()
    dot = lambda a, b: jnp.dot(a, b, preferred_element_type=F32)
    left = halo_in[0]
    right = halo_in[1]
    from_left = dot(left, col_tab[0, 0:128, 128:256]) + dot(left, col_tab[1, 0:128, 128:256])
    from_right = dot(right, col_tab[0, 128:256, 0:128]) + dot(right, col_tab[1, 128:256, 0:128])
    edge_high, edge_low = split(jnp.concatenate([from_left, from_right], axis=1))
    edge = dot3(row_tab[0], row_tab[1], edge_high, edge_low)
    row = jnp.concatenate(
        [row[:, 0:128] + edge[:, 0:128], row[:, 128 : PH - 128], row[:, PH - 128 : PH] + edge[:, 128:256]],
        axis=1,
    )
    squares = row * row / noise_ref[0]
    height = PH // NBAND
    part = height // 2
    for g in range(NBAND):
        term[g] = squares[g * height : (g + 1) * height]
    opposite = lax.rem(band + 2, NBAND)
    near = (above, below)
    far_copy = lambda d: remote(far_out.at[d], far_in.at[d], end_sem.at[2 + d], far_sem.at[d], near[d], "band")
    near_copy = lambda d, n: remote(
        near_out.at[d, n], near_in.at[d, n], end_sem.at[4 + 2 * d + n], near_sem.at[2 * d + n], near[d], "band"
    )
    for d in range(2):
        far_out[d] = term[opposite, d * part : (d + 1) * part].astype(BF16)
        far_copy(d).start()
    for d in range(2):
        near_out[d, 1 - d] = term[near[d], (1 - d) * part : (2 - d) * part].astype(BF16)
        near_copy(d, 1 - d).start()
    for d in range(2):
        far_copy(d).wait_recv()
        near_out[d, d] = (term[near[d], d * part : (d + 1) * part] + far_in[d].astype(F32)).astype(BF16)
        near_copy(d, d).start()
    for n in range(2):
        near_copy(0, n).wait_recv()
        near_copy(1, n).wait_recv()
        own = term[band, n * part : (n + 1) * part]
        chi_ref[n * part : (n + 1) * part] = own + (near_in[0, n].astype(F32) + near_in[1, n].astype(F32))

    for index, ref in enumerate((pair, hop1, hop2)):
        remote(ref, ref, send_sem.at[index], w_sem.at[0], partner).wait_send()
    w_exchange.wait_send()
    for h in range(SIDE - 1):
        w_copy1(h).wait_send()
        w_copy2(h).wait_send()
    to_before.wait_send()
    to_after.wait_send()
    for d in range(2):
        far_copy(d).wait_send()
        for n in range(2):
            near_copy(d, n).wait_send()


def reduce_partials(partial, det_taps, noise_var):
    smem = pl.BlockSpec(memory_space=pltpu.SMEM)
    vmem = pl.BlockSpec(memory_space=pltpu.VMEM)
    dma = pltpu.SemaphoreType.DMA
    height = PH // NBAND
    return pl.pallas_call(
        reduce_kernel,
        out_shape=(
            jax.ShapeDtypeStruct((PH, PH), F32),
            jax.ShapeDtypeStruct((height, PH), F32),
        ),
        in_specs=[vmem, smem, smem],
        out_specs=(vmem, vmem),
        scratch_shapes=[
            pltpu.VMEM((SLOTS, SIDE, SIDE, BLK, BLK), BF16),
            pltpu.VMEM((SLOTS, SIDE - 1, SIDE, BLK, BLK), BF16),
            pltpu.VMEM((SLOTS, SIDE - 1, BLK, BLK), BF16),
            pltpu.VMEM((2, SIDE, SIDE, 8, 128), F32),
            pltpu.VMEM((SIDE, SIDE, 8, 128), F32),
            pltpu.VMEM((2 * SIDE - 2, SIDE, 8, 128), F32),
            pltpu.VMEM((SIDE - 1, SIDE, 8, 128), F32),
            pltpu.VMEM((SIDE - 1, SIDE, 8, 128), F32),
            pltpu.VMEM((2, PH, 128), BF16),
            pltpu.VMEM((2, PH, 128), BF16),
            pltpu.VMEM((2, PH, PH), BF16),
            pltpu.VMEM((2, PH, PH), BF16),
            pltpu.VMEM((PH, PH), BF16),
            pltpu.VMEM((PH, PH), BF16),
            pltpu.VMEM((NBAND, height, PH), F32),
            pltpu.VMEM((2, height // 2, PH), BF16),
            pltpu.VMEM((2, height // 2, PH), BF16),
            pltpu.VMEM((2, 2, height // 2, PH), BF16),
            pltpu.VMEM((2, 2, height // 2, PH), BF16),
            dma((SLOTS, SIDE, SIDE)),
            dma((SLOTS, SIDE - 1, SIDE)),
            dma((SLOTS, SIDE - 1)),
            dma((10,)),
            dma((7,)),
            dma((2,)),
            dma((2,)),
            dma((4,)),
            dma((8,)),
        ],
        compiler_params=pltpu.CompilerParams(
            vmem_limit_bytes=36 << 20, collective_id=0, has_side_effects=True
        ),
        name="reduce_partials",
    )(partial, det_taps, noise_var)


def local(blocks, dest_patch, dest_slot, weights, psf_taps, det_taps, noise_var):
    taps = jnp.pad(psf_taps[0].transpose(1, 0, 2), ((0, 0), (0, 0), (0, 128 - TAPS)))
    partial = match_partials(blocks, dest_patch, dest_slot, weights, taps)
    partial = pltpu.with_memory_space_constraint(partial, pltpu.VMEM)
    image, chi = reduce_partials(partial, det_taps[0], noise_var)
    return image[None], chi


def solution(mesh):
    in_specs = (
        P("band", "patch", None, None),
        P("band", "patch"),
        P("band", "patch"),
        P("band", "patch"),
        P("band", "patch", None, None),
        P("band", None),
        P("band"),
    )
    out_specs = (P("band", None, "patch"), P("band", "patch"))
    return jax.shard_map(local, mesh=mesh, in_specs=in_specs, out_specs=out_specs, check_vma=False)
```

```python
import jax
import jax.numpy as jnp
from jax import lax
from jax.experimental import pallas as pl
from jax.experimental.pallas import tpu as pltpu
from jax.sharding import PartitionSpec as P

DR = 12
DTAPS = 25
SLOTS = 4
TAPS = 41
BLK = 256
PH = 512
NPATCH = 32
NBAND = 4
SIDE = 4
GROUP = 4
STREAMS = ((1, 1), (1, -1), (0, 1), (0, -1))
BF16 = jnp.bfloat16
F32 = jnp.float32


def toeplitz_store(taps_row, matrix):
    rows = jnp.broadcast_to(taps_row, (16, 128))
    skew = pltpu.roll(rows, 0, 1, stride=1, stride_axis=0)
    zeros = jnp.zeros((16, 256), F32)
    wide = jnp.concatenate([zeros, skew, zeros], axis=1)
    for step in range(-9, 3):
        lo = 256 + 16 * step + 20
        tile = wide[:, lo : lo + 128].astype(BF16)
        rb = -step
        if rb >= 0:
            matrix[16 * rb : 16 * rb + 16, 0:128] = tile
        rb = 8 - step
        if rb < 16:
            matrix[16 * rb : 16 * rb + 16, 128:256] = tile


def match_kernel(
    patch_hbm, slot_hbm, weight_hbm, taps_ref, blocks_hbm, out_ref,
    patch_ref, slot_ref, weight_ref, blocks, table_ref, tap_rows, weight_rows, even_mats, odd_mats, sems, small_sems,
):
    count = blocks.shape[0]

    def fetch(g):
        part = pl.ds(g * GROUP, GROUP)
        return pltpu.make_async_copy(blocks_hbm.at[0, part], blocks.at[part], sems.at[g])

    small = [
        pltpu.make_async_copy(src, dst, small_sems.at[n])
        for n, (src, dst) in enumerate(((weight_hbm, weight_ref), (patch_hbm, patch_ref), (slot_hbm, slot_ref)))
    ]
    for copy in small:
        copy.start()
    for g in range(count // GROUP):
        fetch(g).start()
    even_mats[...] = jnp.zeros_like(even_mats)
    odd_mats[...] = jnp.zeros_like(odd_mats)
    table_ref[...] = jnp.zeros_like(table_ref)
    tap_rows[0] = taps_ref[0].astype(F32)
    ends = lax.broadcasted_iota(jnp.int32, (128, 128), 0) + lax.broadcasted_iota(jnp.int32, (128, 128), 1)
    reverse = jnp.where(ends == TAPS - 1, 1.0, 0.0).astype(BF16)
    tap_rows[1] = jnp.dot(taps_ref[1], reverse, preferred_element_type=F32)
    groups = count // GROUP

    def build(g, mats):
        for n in range(GROUP):
            for axis in range(2):
                toeplitz_store(tap_rows[axis, pl.ds(g * GROUP + n, 1), :], mats.at[n, axis])

    build(0, even_mats)
    for copy in small:
        copy.wait()
    diagonal = lax.broadcasted_iota(jnp.int32, (count, count), 0) == lax.broadcasted_iota(jnp.int32, (count, count), 1)
    spread = jnp.where(diagonal, jnp.broadcast_to(weight_ref[...].astype(F32), (count, count)), 0.0)
    weight_rows[...] = jnp.broadcast_to(jnp.sum(spread, axis=1, keepdims=True), (count, 128))

    def match(g, mats, later):
        fetch(g).wait()
        build(lax.min(g + 1, groups - 1), later)
        halves = []
        for n in range(GROUP):
            half = jnp.dot(mats[n, 0], blocks[g * GROUP + n], preferred_element_type=F32)
            halves.append(half.astype(BF16))
        for n in range(GROUP):
            i = g * GROUP + n
            full = jnp.dot(halves[n], mats[n, 1], preferred_element_type=F32).astype(BF16)
            weight = weight_rows[pl.ds(i, 1), :]
            patch = patch_ref[0, i]
            slot = slot_ref[0, i]
            place = (patch & 1) * (SIDE * SIDE) + ((patch >> 1) & (SIDE - 1)) * SIDE + (patch >> 3)
            before = table_ref[place, pl.ds(slot, 1), :]
            table_ref[place, pl.ds(slot, 1), :] = before + weight
            wide = lambda row: jnp.broadcast_to(jnp.concatenate([row, row], axis=1), (BLK, BLK))
            tile = patch * SLOTS + slot
            old = jnp.where(wide(before) > 0.0, out_ref[tile].astype(F32), 0.0)
            out_ref[tile] = (old + wide(weight) * full.astype(F32)).astype(BF16)

    @pl.loop(0, groups // 2)
    def _(pair):
        match(2 * pair, even_mats, odd_mats)
        match(2 * pair + 1, odd_mats, even_mats)

    high, low = split(table_ref[...].reshape(NPATCH * 8, 128))
    out_ref[NPATCH * SLOTS, :, 0:128] = high
    out_ref[NPATCH * SLOTS, :, 128:256] = low


def match_partials(blocks, dest_patch, dest_slot, weights, taps):
    count = blocks.shape[1]
    hbm = pl.BlockSpec(memory_space=pltpu.HBM)
    vmem = pl.BlockSpec(memory_space=pltpu.VMEM)
    keep = lambda x: pltpu.with_memory_space_constraint(x, pltpu.HBM)
    return pl.pallas_call(
        match_kernel,
        out_shape=pltpu.VMEM((NPATCH * SLOTS + 1, BLK, BLK), BF16),
        in_specs=[hbm, hbm, hbm, vmem, hbm],
        out_specs=vmem,
        scratch_shapes=[
            pltpu.SMEM((1, count), jnp.int32),
            pltpu.SMEM((1, count), jnp.int32),
            pltpu.VMEM((1, count), BF16),
            pltpu.VMEM((count, BLK, BLK), BF16),
            pltpu.VMEM((NPATCH, 8, 128), F32),
            pltpu.VMEM((2, count, 128), F32),
            pltpu.VMEM((count, 128), F32),
            pltpu.VMEM((GROUP, 2, BLK, BLK), BF16),
            pltpu.VMEM((GROUP, 2, BLK, BLK), BF16),
            pltpu.SemaphoreType.DMA((count // GROUP,)),
            pltpu.SemaphoreType.DMA((3,)),
        ],
        compiler_params=pltpu.CompilerParams(vmem_limit_bytes=28 << 20),
        name="match_partials",
    )(keep(dest_patch), keep(dest_slot), keep(weights), taps, keep(blocks))


def wrap(x):
    return lax.rem(x + 2 * SIDE, SIDE)


def patch_index(y, z, core):
    return (y * SIDE + z) * 2 + core


def split(x):
    high = x.astype(BF16)
    return high, (x - high.astype(F32)).astype(BF16)


def dot3(ah, al, bh, bl):
    dot = lambda a, b: jnp.dot(a, b, preferred_element_type=F32)
    return dot(ah, bh) + (dot(ah, bl) + dot(al, bh))


def tap_block(det_ref, shift, sign):
    offset = lax.broadcasted_iota(jnp.int32, (128, 128), 1) - lax.broadcasted_iota(jnp.int32, (128, 128), 0)
    offset = sign * offset + shift + DR
    block = jnp.zeros((128, 128), F32)
    for t in range(DTAPS):
        block = jnp.where(offset == t, det_ref[t], block)
    return block


def build_tables(det_ref, col_tab, row_tab):
    col_tab[...] = jnp.zeros_like(col_tab)
    row_tab[...] = jnp.zeros_like(row_tab)
    for sign in (1, -1):
        for diag in (-1, 0, 1):
            high, low = split(tap_block(det_ref, sign * 128 * diag, sign))
            for rb in range(PH // 128):
                cb = rb + diag
                if 0 <= cb < PH // 128:
                    for n, part in enumerate((high, low)):
                        if sign == 1:
                            row_tab[n, rb, :, 128 * cb : 128 * cb + 128] = part
                        else:
                            col_tab[n, 128 * rb : 128 * rb + 128, 128 * cb : 128 * cb + 128] = part


def reduce_kernel(
    d_ref, det_ref, noise_ref, img_ref, chi_ref,
    pair, hop1, hop2, w_ref, w_pair, w_acc, w_hop1, w_hop2, halo_out, halo_in, col_tab, row_tab, high, low,
    term, far_out, far_in, near_out, near_in,
    pair_sem, hop1_sem, hop2_sem, send_sem, w_sem, halo_sem, far_sem, near_sem, end_sem,
):
    me = lax.axis_index("patch")
    band = lax.axis_index("band")
    core = lax.rem(me, 2)
    place = (lax.div(me, 2 * SIDE), lax.rem(lax.div(me, 2), SIDE))
    partner = me + 1 - 2 * core
    before = lax.rem(me + NPATCH - 1, NPATCH)
    after = lax.rem(me + 1, NPATCH)
    beside = lax.rem(me + NPATCH - 1 + 2 * core, NPATCH)

    def moved(axis, step):
        there = list(place)
        there[axis] = wrap(place[axis] + step)
        return patch_index(there[0], there[1], core)

    barrier = pltpu.get_barrier_semaphore()
    for device in (partner, beside, moved(0, 1), moved(0, -1), moved(1, 1), moved(1, -1)):
        pl.semaphore_signal(barrier, inc=1, device_id={"patch": device})
    above = lax.rem(band + 1, NBAND)
    below = lax.rem(band + NBAND - 1, NBAND)
    for device in (above, below):
        pl.semaphore_signal(barrier, inc=1, device_id={"band": device})
    pl.semaphore_wait(barrier, 8)

    def remote(src, dst, send, recv, device, axis="patch"):
        return pltpu.make_async_remote_copy(
            src_ref=src, dst_ref=dst, send_sem=send, recv_sem=recv, device_id={axis: device}
        )

    def dest(s, h, k):
        axis, step = STREAMS[s]
        first = wrap(place[axis] - step * (1 + h))
        other = wrap(place[1 - axis] - step * (1 + k))
        return (first, other) if axis == 0 else (other, first)

    def tile(s, h, k, parity):
        y, z = dest(s, h, k)
        return patch_index(y, z, parity) * SLOTS + s

    next1 = [moved(axis, step) for axis, step in STREAMS]
    next2 = [moved(1 - axis, step) for axis, step in STREAMS]

    def send_pair(s, h, k):
        remote(
            d_ref.at[tile(s, h, k, 1 - core)], pair.at[s, h, k], send_sem.at[0], pair_sem.at[s, h, k], partner
        ).start()

    def wait_pair(s, h, k):
        remote(pair.at[s, h, k], pair.at[s, h, k], send_sem.at[0], pair_sem.at[s, h, k], partner).wait_recv()

    def hop1_copy(s, h, k):
        return remote(pair.at[s, h, k], hop1.at[s, h, k], send_sem.at[1], hop1_sem.at[s, h, k], next1[s])

    def hop2_copy(s, k):
        return remote(pair.at[s, 3, k], hop2.at[s, k], send_sem.at[2], hop2_sem.at[s, k], next2[s])

    table = d_ref[NPATCH * SLOTS]
    table = table[:, 0:128].astype(F32) + table[:, 128:256].astype(F32)
    w_ref[...] = table.reshape(2, SIDE, SIDE, 8, 128)
    w_exchange = remote(w_ref.at[1 - core], w_pair, send_sem.at[3], w_sem.at[0], partner)
    w_exchange.start()

    def send_pairs(h, first):
        @pl.loop(first, first + 2)
        def _(k):
            for s in range(SLOTS):
                send_pair(s, h, k)

    send_pairs(0, 0)
    w_exchange.wait_recv()

    def w_here(h):
        z = wrap(place[1] - 1 - h)
        return w_ref[core, z] + w_pair[z]

    def w_copy1(h):
        return remote(w_acc.at[h], w_hop1.at[h], send_sem.at[4 + h], w_sem.at[1 + h], moved(1, 1))

    def w_copy2(k):
        return remote(w_acc.at[3 + k], w_hop2.at[k], send_sem.at[7 + k], w_sem.at[4 + k], moved(0, 1))

    def here(s, h, k):
        y, z = dest(s, h, k)
        wide = lambda row: jnp.broadcast_to(jnp.concatenate([row, row], axis=1), (BLK, BLK))
        mine = jnp.where(
            wide(w_ref[core, z, y, s : s + 1]) > 0.0, d_ref[tile(s, h, k, core)].astype(F32), 0.0
        )
        other = jnp.where(wide(w_pair[z, y, s : s + 1]) > 0.0, pair[s, h, k].astype(F32), 0.0)
        return mine + other

    def start_units(first, *ahead):
        @pl.loop(first, first + 2)
        def _(k):
            for later, start in ahead:
                for s in range(SLOTS):
                    send_pair(s, later, k - first + start)
            for s in range(SLOTS):
                wait_pair(s, 0, k)
                pair[s, 0, k] = here(s, 0, k).astype(BF16)
                hop1_copy(s, 0, k).start()

    def pass_units(h, first, *ahead):
        @pl.loop(first, first + 2)
        def _(k):
            for later, start in ahead:
                for s in range(SLOTS):
                    send_pair(s, later, k - first + start)
            for s in range(SLOTS):
                wait_pair(s, h, k)
                total = here(s, h, k)
                hop1_copy(s, h - 1, k).wait_recv()
                pair[s, h, k] = (total + hop1[s, h - 1, k].astype(F32)).astype(BF16)
                hop1_copy(s, h, k).start()

    def gathered(s, k):
        wait_pair(s, 3, k)
        hop1_copy(s, 2, k).wait_recv()
        return here(s, 3, k) + hop1[s, 2, k].astype(F32)

    def turn_units(k):
        for s in range(SLOTS):
            total = gathered(s, k)
            if k > 0:
                hop2_copy(s, k - 1).wait_recv()
                total = total + hop2[s, k - 1].astype(F32)
            pair[s, 3, k] = total.astype(BF16)
            hop2_copy(s, k).start()

    def w_step(n):
        if n > 0:
            (w_copy1(n - 1) if n < 4 else w_copy2(n - 4)).wait_recv()
        if n < 3:
            w_acc[n] = w_here(n) + w_hop1[n - 1] if n > 0 else w_here(n)
            w_copy1(n).start()
        else:
            w_acc[n] = w_here(3) + w_hop1[2] if n == 3 else w_acc[3] + w_hop2[n - 4]
            w_copy2(n - 3).start()

    w_step(0)
    start_units(0, (1, 0))
    build_tables(det_ref, col_tab, row_tab)
    pass_units(1, 0, (2, 0))
    w_step(1)
    pass_units(2, 0, (0, 2))
    w_step(2)
    start_units(2, (3, 0), (1, 2))
    w_step(3)
    turn_units(0)
    pass_units(1, 2, (2, 2))
    w_step(4)
    turn_units(1)
    pass_units(2, 2, (3, 2))
    w_step(5)
    turn_units(2)
    w_copy2(2).wait_recv()
    weight_sum = w_acc[3, place[0]] + w_hop2[2, place[0]]
    scale = 1.0 / jnp.maximum(weight_sum, 1.0)

    def halo_copy(d, half):
        rows = pl.ds(half * BLK, BLK)
        device = after if d == 0 else before
        return remote(
            halo_out.at[d, rows], halo_in.at[d, rows], end_sem.at[2 * half + d], halo_sem.at[2 * half + d], device
        )

    for half in range(2):
        rows = slice(half * BLK, (half + 1) * BLK)
        for s in (2 * half, 2 * half + 1):
            total = gathered(s, 3)
            hop2_copy(s, 2).wait_recv()
            value = (total + hop2[s, 2].astype(F32)) * jnp.broadcast_to(scale[s : s + 1, 0:1], (BLK, BLK))
            cols = slice((s % 2) * BLK, (s % 2 + 1) * BLK)
            img_ref[rows, cols] = value
            high[rows, cols], low[rows, cols] = split(value)
        halo_out[0, rows] = high[rows, PH - 128 : PH]
        halo_out[1, rows] = high[rows, 0:128]
        for d in range(2):
            halo_copy(d, half).start()

    high[...], low[...] = split(dot3(high[...], low[...], col_tab[0], col_tab[1]))
    for half in range(2):
        for d in range(2):
            halo_copy(d, half).wait_recv()
    dot = lambda a, b: jnp.dot(a, b, preferred_element_type=F32)
    left = halo_in[0]
    right = halo_in[1]
    from_left = dot(left, col_tab[0, 0:128, 128:256]) + dot(left, col_tab[1, 0:128, 128:256])
    from_right = dot(right, col_tab[0, 128:256, 0:128]) + dot(right, col_tab[1, 128:256, 0:128])
    edge_high, edge_low = split(jnp.concatenate([from_left, from_right], axis=1))
    height = PH // NBAND
    part = height // 2
    opposite = lax.rem(band + 2, NBAND)
    near = (above, below)
    over_noise = (1.0 / jnp.full((8, 128), noise_ref[0], F32))[0:1, 0:1]

    def rows_of(first, chunks):
        row_high = jnp.concatenate([row_tab[0, g] for g in chunks], axis=0)
        row_low = jnp.concatenate([row_tab[1, g] for g in chunks], axis=0)
        row = dot3(row_high, row_low, high[...], low[...])
        edge = dot3(row_high, row_low, edge_high, edge_low)
        row = jnp.concatenate(
            [row[:, 0:128] + edge[:, 0:128], row[:, 128 : PH - 128], row[:, PH - 128 : PH] + edge[:, 128:256]],
            axis=1,
        )
        squares = row * row * jnp.broadcast_to(over_noise, row.shape)
        for n in range(len(chunks)):
            term[first + n] = squares[n * height : (n + 1) * height]

    far_copy = lambda d: remote(far_out.at[d], far_in.at[d], end_sem.at[4 + d], far_sem.at[d], near[d], "band")
    near_copy = lambda d, n: remote(
        near_out.at[d, n], near_in.at[d, n], end_sem.at[6 + 2 * d + n], near_sem.at[2 * d + n], near[d], "band"
    )

    def send_early(d):
        near_out[d, 1 - d] = term[1 + d, (1 - d) * part : (2 - d) * part].astype(BF16)
        near_copy(d, 1 - d).start()

    rows_of(0, (opposite, above))
    for d in range(2):
        far_out[d] = term[0, d * part : (d + 1) * part].astype(BF16)
        far_copy(d).start()
    send_early(0)
    rows_of(2, (below, band))
    send_early(1)
    for d in range(2):
        far_copy(d).wait_recv()
        near_out[d, d] = (term[1 + d, d * part : (d + 1) * part] + far_in[d].astype(F32)).astype(BF16)
        near_copy(d, d).start()
    for n in range(2):
        near_copy(0, n).wait_recv()
        near_copy(1, n).wait_recv()
        own = term[3, n * part : (n + 1) * part]
        chi_ref[n * part : (n + 1) * part] = own + (near_in[0, n].astype(F32) + near_in[1, n].astype(F32))

    for index, ref in enumerate((pair, hop1, hop2)):
        remote(ref, ref, send_sem.at[index], w_sem.at[0], partner).wait_send()
    w_exchange.wait_send()
    for h in range(SIDE - 1):
        w_copy1(h).wait_send()
        w_copy2(h).wait_send()
    for half in range(2):
        for d in range(2):
            halo_copy(d, half).wait_send()
    for d in range(2):
        far_copy(d).wait_send()
        for n in range(2):
            near_copy(d, n).wait_send()


def reduce_partials(partial, det_taps, noise_var):
    smem = pl.BlockSpec(memory_space=pltpu.SMEM)
    vmem = pl.BlockSpec(memory_space=pltpu.VMEM)
    dma = pltpu.SemaphoreType.DMA
    height = PH // NBAND
    return pl.pallas_call(
        reduce_kernel,
        out_shape=(
            jax.ShapeDtypeStruct((PH, PH), F32),
            jax.ShapeDtypeStruct((height, PH), F32),
        ),
        in_specs=[vmem, smem, smem],
        out_specs=(vmem, vmem),
        scratch_shapes=[
            pltpu.VMEM((SLOTS, SIDE, SIDE, BLK, BLK), BF16),
            pltpu.VMEM((SLOTS, SIDE - 1, SIDE, BLK, BLK), BF16),
            pltpu.VMEM((SLOTS, SIDE - 1, BLK, BLK), BF16),
            pltpu.VMEM((2, SIDE, SIDE, 8, 128), F32),
            pltpu.VMEM((SIDE, SIDE, 8, 128), F32),
            pltpu.VMEM((2 * SIDE - 2, SIDE, 8, 128), F32),
            pltpu.VMEM((SIDE - 1, SIDE, 8, 128), F32),
            pltpu.VMEM((SIDE - 1, SIDE, 8, 128), F32),
            pltpu.VMEM((2, PH, 128), BF16),
            pltpu.VMEM((2, PH, 128), BF16),
            pltpu.VMEM((2, PH, PH), BF16),
            pltpu.VMEM((2, PH // 128, 128, PH), BF16),
            pltpu.VMEM((PH, PH), BF16),
            pltpu.VMEM((PH, PH), BF16),
            pltpu.VMEM((NBAND, height, PH), F32),
            pltpu.VMEM((2, height // 2, PH), BF16),
            pltpu.VMEM((2, height // 2, PH), BF16),
            pltpu.VMEM((2, 2, height // 2, PH), BF16),
            pltpu.VMEM((2, 2, height // 2, PH), BF16),
            dma((SLOTS, SIDE, SIDE)),
            dma((SLOTS, SIDE - 1, SIDE)),
            dma((SLOTS, SIDE - 1)),
            dma((10,)),
            dma((7,)),
            dma((4,)),
            dma((2,)),
            dma((4,)),
            dma((10,)),
        ],
        compiler_params=pltpu.CompilerParams(
            vmem_limit_bytes=36 << 20, collective_id=0, has_side_effects=True
        ),
        name="reduce_partials",
    )(partial, det_taps, noise_var)


def local(blocks, dest_patch, dest_slot, weights, psf_taps, det_taps, noise_var):
    taps = jnp.pad(psf_taps[0].transpose(1, 0, 2), ((0, 0), (0, 0), (0, 128 - TAPS)))
    partial = match_partials(blocks, dest_patch, dest_slot, weights, taps)
    partial = pltpu.with_memory_space_constraint(partial, pltpu.VMEM)
    image, chi = reduce_partials(partial, det_taps[0], noise_var)
    return image[None], chi


def solution(mesh):
    in_specs = (
        P("band", "patch", None, None),
        P("band", "patch"),
        P("band", "patch"),
        P("band", "patch"),
        P("band", "patch", None, None),
        P("band", None),
        P("band"),
    )
    out_specs = (P("band", None, "patch"), P("band", "patch"))
    return jax.shard_map(local, mesh=mesh, in_specs=in_specs, out_specs=out_specs, check_vma=False)
```

```python
import jax
import jax.numpy as jnp
from jax import lax
from jax.experimental import pallas as pl
from jax.experimental.pallas import tpu as pltpu
from jax.sharding import PartitionSpec as P

DR = 12
DTAPS = 25
SLOTS = 4
TAPS = 41
BLK = 256
HALF = 128
PH = 512
NPATCH = 32
NBAND = 4
SIDE = 4
GROUP = 4
STREAMS = ((1, 1), (1, -1), (0, 1), (0, -1))
BF16 = jnp.bfloat16
F32 = jnp.float32


def toeplitz_store(taps_row, matrix):
    rows = jnp.broadcast_to(taps_row, (16, 128))
    skew = pltpu.roll(rows, 0, 1, stride=1, stride_axis=0)
    zeros = jnp.zeros((16, 256), F32)
    wide = jnp.concatenate([zeros, skew, zeros], axis=1)
    for step in range(-9, 3):
        lo = 256 + 16 * step + 20
        tile = wide[:, lo : lo + 128].astype(BF16)
        rb = -step
        if rb >= 0:
            matrix[16 * rb : 16 * rb + 16, 0:128] = tile
        rb = 8 - step
        if rb < 16:
            matrix[16 * rb : 16 * rb + 16, 128:256] = tile


def match_kernel(
    patch_hbm, slot_hbm, weight_hbm, taps_hbm, blocks_hbm, out_ref,
    patch_ref, slot_ref, weight_ref, taps_ref, blocks, table_ref, tap_rows, weight_rows, even_mats, odd_mats, sems, small_sems,
):
    count = blocks.shape[0]

    def fetch(g):
        part = pl.ds(g * GROUP, GROUP)
        return pltpu.make_async_copy(blocks_hbm.at[0, part], blocks.at[part], sems.at[g])

    small = [
        pltpu.make_async_copy(src, dst, small_sems.at[n])
        for n, (src, dst) in enumerate(
            ((taps_hbm, taps_ref), (weight_hbm, weight_ref), (patch_hbm, patch_ref), (slot_hbm, slot_ref))
        )
    ]
    for copy in small:
        copy.start()
    for g in range(count // GROUP):
        fetch(g).start()
    even_mats[...] = jnp.zeros_like(even_mats)
    odd_mats[...] = jnp.zeros_like(odd_mats)
    table_ref[...] = jnp.zeros_like(table_ref)
    small[0].wait()
    raw = taps_ref[0].astype(F32).reshape(2 * count, TAPS).astype(BF16)
    from_tap = lax.broadcasted_iota(jnp.int32, (TAPS, 128), 0)
    to_lane = lax.broadcasted_iota(jnp.int32, (TAPS, 128), 1)
    for axis, picks in enumerate((from_tap == to_lane, from_tap + to_lane == TAPS - 1)):
        tap_rows[axis] = jnp.dot(raw, jnp.where(picks, 1.0, 0.0).astype(BF16), preferred_element_type=F32)
    groups = count // GROUP

    def build(g, mats):
        for n in range(GROUP):
            for axis in range(2):
                toeplitz_store(tap_rows[axis, pl.ds(2 * (g * GROUP + n) + axis, 1), :], mats.at[n, axis])

    build(0, even_mats)
    for copy in small[1:]:
        copy.wait()
    diagonal = lax.broadcasted_iota(jnp.int32, (count, count), 0) == lax.broadcasted_iota(jnp.int32, (count, count), 1)
    spread = jnp.where(diagonal, jnp.broadcast_to(weight_ref[...].astype(F32), (count, count)), 0.0)
    weight_rows[...] = jnp.broadcast_to(jnp.sum(spread, axis=1, keepdims=True), (count, 128))

    def match(g, mats, later):
        fetch(g).wait()
        build(lax.min(g + 1, groups - 1), later)
        halves = []
        for n in range(GROUP):
            half = jnp.dot(mats[n, 0], blocks[g * GROUP + n], preferred_element_type=F32)
            halves.append(half.astype(BF16))
        for n in range(GROUP):
            i = g * GROUP + n
            full = jnp.dot(halves[n], mats[n, 1], preferred_element_type=F32).astype(BF16)
            weight = weight_rows[pl.ds(i, 1), :]
            patch = patch_ref[0, i]
            slot = slot_ref[0, i]
            place = (patch & 1) * (SIDE * SIDE) + ((patch >> 1) & (SIDE - 1)) * SIDE + (patch >> 3)
            before = table_ref[place, pl.ds(slot, 1), :]
            table_ref[place, pl.ds(slot, 1), :] = before + weight
            wide = lambda row: jnp.broadcast_to(jnp.concatenate([row, row], axis=1), (BLK, BLK))
            tile = patch * SLOTS + slot
            old = jnp.where(wide(before) > 0.0, out_ref[tile].astype(F32), 0.0)
            out_ref[tile] = (old + wide(weight) * full.astype(F32)).astype(BF16)

    @pl.loop(0, groups // 2)
    def _(pair):
        match(2 * pair, even_mats, odd_mats)
        match(2 * pair + 1, odd_mats, even_mats)

    high, low = split(table_ref[...].reshape(NPATCH * 8, 128))
    out_ref[NPATCH * SLOTS, :, 0:128] = high
    out_ref[NPATCH * SLOTS, :, 128:256] = low


def match_partials(blocks, dest_patch, dest_slot, weights, taps):
    count = blocks.shape[1]
    hbm = pl.BlockSpec(memory_space=pltpu.HBM)
    vmem = pl.BlockSpec(memory_space=pltpu.VMEM)
    keep = lambda x: pltpu.with_memory_space_constraint(x, pltpu.HBM)
    return pl.pallas_call(
        match_kernel,
        out_shape=pltpu.VMEM((NPATCH * SLOTS + 1, BLK, BLK), BF16),
        in_specs=[hbm] * 5,
        out_specs=vmem,
        scratch_shapes=[
            pltpu.SMEM((1, count), jnp.int32),
            pltpu.SMEM((1, count), jnp.int32),
            pltpu.VMEM((1, count), BF16),
            pltpu.VMEM(taps.shape, BF16),
            pltpu.VMEM((count, BLK, BLK), BF16),
            pltpu.VMEM((NPATCH, 8, 128), F32),
            pltpu.VMEM((2, 2 * count, 128), F32),
            pltpu.VMEM((count, 128), F32),
            pltpu.VMEM((GROUP, 2, BLK, BLK), BF16),
            pltpu.VMEM((GROUP, 2, BLK, BLK), BF16),
            pltpu.SemaphoreType.DMA((count // GROUP,)),
            pltpu.SemaphoreType.DMA((4,)),
        ],
        compiler_params=pltpu.CompilerParams(vmem_limit_bytes=28 << 20),
        name="match_partials",
    )(*(keep(x) for x in (dest_patch, dest_slot, weights, taps, blocks)))


def wrap(x):
    return lax.rem(x + 2 * SIDE, SIDE)


def patch_index(y, z, core):
    return (y * SIDE + z) * 2 + core


def split(x):
    high = x.astype(BF16)
    return high, (x - high.astype(F32)).astype(BF16)


def dot3(ah, al, bh, bl):
    dot = lambda a, b: jnp.dot(a, b, preferred_element_type=F32)
    return dot(ah, bh) + (dot(ah, bl) + dot(al, bh))


def tap_block(det_ref, shift, sign):
    offset = lax.broadcasted_iota(jnp.int32, (128, 128), 1) - lax.broadcasted_iota(jnp.int32, (128, 128), 0)
    offset = sign * offset + shift + DR
    block = jnp.zeros((128, 128), F32)
    for t in range(DTAPS):
        block = jnp.where(offset == t, det_ref[t], block)
    return block


def build_tables(det_ref, col_tab, row_tab):
    col_tab[...] = jnp.zeros_like(col_tab)
    row_tab[...] = jnp.zeros_like(row_tab)
    for sign in (1, -1):
        for diag in (-1, 0, 1):
            high, low = split(tap_block(det_ref, sign * 128 * diag, sign))
            for rb in range(PH // 128):
                cb = rb + diag
                if 0 <= cb < PH // 128:
                    for n, part in enumerate((high, low)):
                        if sign == 1:
                            row_tab[n, rb, :, 128 * cb : 128 * cb + 128] = part
                        else:
                            col_tab[n, 128 * rb : 128 * rb + 128, 128 * cb : 128 * cb + 128] = part


def reduce_kernel(
    d_ref, det_ref, noise_ref, img_ref, chi_ref,
    pair, hop1, hop2, w_ref, w_pair, w_acc, w_hop1, w_hop2, halo_out, halo_in, col_tab, row_tab, high, low,
    term, far_out, far_in, near_out, near_in,
    pair_sem, hop1_sem, hop2_sem, send_sem, w_sem, halo_sem, far_sem, near_sem, end_sem,
):
    me = lax.axis_index("patch")
    band = lax.axis_index("band")
    core = lax.rem(me, 2)
    place = (lax.div(me, 2 * SIDE), lax.rem(lax.div(me, 2), SIDE))
    partner = me + 1 - 2 * core
    before = lax.rem(me + NPATCH - 1, NPATCH)
    after = lax.rem(me + 1, NPATCH)
    beside = lax.rem(me + NPATCH - 1 + 2 * core, NPATCH)

    def moved(axis, step):
        there = list(place)
        there[axis] = wrap(place[axis] + step)
        return patch_index(there[0], there[1], core)

    barrier = pltpu.get_barrier_semaphore()
    for device in (partner, beside, moved(0, 1), moved(0, -1), moved(1, 1), moved(1, -1)):
        pl.semaphore_signal(barrier, inc=1, device_id={"patch": device})
    above = lax.rem(band + 1, NBAND)
    below = lax.rem(band + NBAND - 1, NBAND)
    for device in (above, below):
        pl.semaphore_signal(barrier, inc=1, device_id={"band": device})
    pl.semaphore_wait(barrier, 8)

    def remote(src, dst, send, recv, device, axis="patch"):
        return pltpu.make_async_remote_copy(
            src_ref=src, dst_ref=dst, send_sem=send, recv_sem=recv, device_id={axis: device}
        )

    def dest(s, h, k):
        axis, step = STREAMS[s]
        first = wrap(place[axis] - step * (1 + h))
        other = wrap(place[1 - axis] - step * (1 + k))
        return (first, other) if axis == 0 else (other, first)

    def tile(s, h, k, parity):
        y, z = dest(s, h, k)
        return patch_index(y, z, parity) * SLOTS + s

    next1 = [moved(axis, step) for axis, step in STREAMS]
    next2 = [moved(1 - axis, step) for axis, step in STREAMS]

    def send_pair(s, h, k):
        remote(
            d_ref.at[tile(s, h, k, 1 - core)], pair.at[s, h, k], send_sem.at[0], pair_sem.at[s, h, k], partner
        ).start()

    def wait_pair(s, h, k):
        remote(pair.at[s, h, k], pair.at[s, h, k], send_sem.at[0], pair_sem.at[s, h, k], partner).wait_recv()

    def hop1_copy(s, h, k):
        return remote(pair.at[s, h, k], hop1.at[s, h, k], send_sem.at[1], hop1_sem.at[s, h, k], next1[s])

    def hop2_copy(s, k, sub):
        rows = pl.ds(sub * HALF, HALF)
        return remote(
            pair.at[s, 3, k, rows], hop2.at[s, k, rows], send_sem.at[2], hop2_sem.at[s, k, sub], next2[s]
        )

    table = d_ref[NPATCH * SLOTS]
    table = table[:, 0:128].astype(F32) + table[:, 128:256].astype(F32)
    w_ref[...] = table.reshape(2, SIDE, SIDE, 8, 128)
    w_exchange = remote(w_ref.at[1 - core], w_pair, send_sem.at[3], w_sem.at[0], partner)
    w_exchange.start()

    def send_pairs(h, first):
        @pl.loop(first, first + 2)
        def _(k):
            for s in range(SLOTS):
                send_pair(s, h, k)

    send_pairs(0, 0)
    w_exchange.wait_recv()

    def w_here(h):
        z = wrap(place[1] - 1 - h)
        return w_ref[core, z] + w_pair[z]

    def w_copy1(h):
        return remote(w_acc.at[h], w_hop1.at[h], send_sem.at[4 + h], w_sem.at[1 + h], moved(1, 1))

    def w_copy2(k):
        return remote(w_acc.at[3 + k], w_hop2.at[k], send_sem.at[7 + k], w_sem.at[4 + k], moved(0, 1))

    def here(s, h, k, rows=slice(0, BLK)):
        y, z = dest(s, h, k)
        height = rows.stop - rows.start
        wide = lambda row: jnp.broadcast_to(jnp.concatenate([row, row], axis=1), (height, BLK))
        mine = jnp.where(
            wide(w_ref[core, z, y, s : s + 1]) > 0.0, d_ref[tile(s, h, k, core), rows].astype(F32), 0.0
        )
        other = jnp.where(wide(w_pair[z, y, s : s + 1]) > 0.0, pair[s, h, k, rows].astype(F32), 0.0)
        return mine + other

    def start_units(first, *ahead):
        @pl.loop(first, first + 2)
        def _(k):
            for later, start in ahead:
                for s in range(SLOTS):
                    send_pair(s, later, k - first + start)
            for s in range(SLOTS):
                wait_pair(s, 0, k)
                pair[s, 0, k] = here(s, 0, k).astype(BF16)
                hop1_copy(s, 0, k).start()

    def pass_units(h, first, *ahead):
        @pl.loop(first, first + 2)
        def _(k):
            for later, start in ahead:
                for s in range(SLOTS):
                    send_pair(s, later, k - first + start)
            for s in range(SLOTS):
                wait_pair(s, h, k)
                total = here(s, h, k)
                hop1_copy(s, h - 1, k).wait_recv()
                pair[s, h, k] = (total + hop1[s, h - 1, k].astype(F32)).astype(BF16)
                hop1_copy(s, h, k).start()

    def gathered(s, k, sub):
        rows = slice(sub * HALF, (sub + 1) * HALF)
        if sub == 0:
            wait_pair(s, 3, k)
            hop1_copy(s, 2, k).wait_recv()
        total = here(s, 3, k, rows) + hop1[s, 2, k, rows].astype(F32)
        if k > 0:
            hop2_copy(s, k - 1, sub).wait_recv()
            total = total + hop2[s, k - 1, rows].astype(F32)
        return total

    def turn_units(k):
        for sub in range(2):
            for s in range(SLOTS):
                pair[s, 3, k, sub * HALF : (sub + 1) * HALF] = gathered(s, k, sub).astype(BF16)
                hop2_copy(s, k, sub).start()

    def w_step(n):
        if n > 0:
            (w_copy1(n - 1) if n < 4 else w_copy2(n - 4)).wait_recv()
        if n < 3:
            w_acc[n] = w_here(n) + w_hop1[n - 1] if n > 0 else w_here(n)
            w_copy1(n).start()
        else:
            w_acc[n] = w_here(3) + w_hop1[2] if n == 3 else w_acc[3] + w_hop2[n - 4]
            w_copy2(n - 3).start()

    w_step(0)
    start_units(0, (1, 0))
    build_tables(det_ref, col_tab, row_tab)
    pass_units(1, 0, (2, 0))
    w_step(1)
    pass_units(2, 0, (0, 2))
    w_step(2)
    start_units(2, (3, 0), (1, 2))
    w_step(3)
    turn_units(0)
    pass_units(1, 2, (2, 2))
    w_step(4)
    turn_units(1)
    pass_units(2, 2, (3, 2))
    w_step(5)
    turn_units(2)
    w_copy2(2).wait_recv()
    weight_sum = w_acc[3, place[0]] + w_hop2[2, place[0]]
    scale = 1.0 / jnp.maximum(weight_sum, 1.0)

    def halo_copy(d, sub):
        device = after if d == 0 else before
        return remote(
            halo_out.at[d, sub], halo_in.at[d, sub], end_sem.at[2 * sub + d], halo_sem.at[2 * sub + d], device
        )

    for sub in range(2):
        for s in range(SLOTS):
            value = gathered(s, 3, sub) * jnp.broadcast_to(scale[s : s + 1, 0:1], (HALF, BLK))
            top = (s // 2) * BLK + sub * HALF
            rows = slice(top, top + HALF)
            cols = slice((s % 2) * BLK, (s % 2 + 1) * BLK)
            img_ref[rows, cols] = value
            high[rows, cols], low[rows, cols] = split(value)
        for half in range(2):
            top = half * BLK + sub * HALF
            rows = slice(top, top + HALF)
            halo_out[0, sub, half] = high[rows, PH - 128 : PH]
            halo_out[1, sub, half] = high[rows, 0:128]
        for d in range(2):
            halo_copy(d, sub).start()

    high[...], low[...] = split(dot3(high[...], low[...], col_tab[0], col_tab[1]))
    for sub in range(2):
        for d in range(2):
            halo_copy(d, sub).wait_recv()
    dot = lambda a, b: jnp.dot(a, b, preferred_element_type=F32)
    sides = [jnp.concatenate([halo_in[d, n % 2, n // 2] for n in range(4)], axis=0) for d in range(2)]
    left, right = sides
    from_left = dot(left, col_tab[0, 0:128, 128:256]) + dot(left, col_tab[1, 0:128, 128:256])
    from_right = dot(right, col_tab[0, 128:256, 0:128]) + dot(right, col_tab[1, 128:256, 0:128])
    edge_high, edge_low = split(jnp.concatenate([from_left, from_right], axis=1))
    height = PH // NBAND
    part = height // 2
    opposite = lax.rem(band + 2, NBAND)
    near = (above, below)
    over_noise = (1.0 / jnp.full((8, 128), noise_ref[0], F32))[0:1, 0:1]

    def rows_of(first, chunks):
        row_high = jnp.concatenate([row_tab[0, g] for g in chunks], axis=0)
        row_low = jnp.concatenate([row_tab[1, g] for g in chunks], axis=0)
        row = dot3(row_high, row_low, high[...], low[...])
        edge = dot3(row_high, row_low, edge_high, edge_low)
        row = jnp.concatenate(
            [row[:, 0:128] + edge[:, 0:128], row[:, 128 : PH - 128], row[:, PH - 128 : PH] + edge[:, 128:256]],
            axis=1,
        )
        squares = row * row * jnp.broadcast_to(over_noise, row.shape)
        for n in range(len(chunks)):
            term[first + n] = squares[n * height : (n + 1) * height]

    far_copy = lambda d: remote(far_out.at[d], far_in.at[d], end_sem.at[4 + d], far_sem.at[d], near[d], "band")
    near_copy = lambda d, n: remote(
        near_out.at[d, n], near_in.at[d, n], end_sem.at[6 + 2 * d + n], near_sem.at[2 * d + n], near[d], "band"
    )

    def send_early(d):
        near_out[d, 1 - d] = term[1 + d, (1 - d) * part : (2 - d) * part].astype(BF16)
        near_copy(d, 1 - d).start()

    rows_of(0, (opposite, above))
    for d in range(2):
        far_out[d] = term[0, d * part : (d + 1) * part].astype(BF16)
        far_copy(d).start()
    send_early(0)
    rows_of(2, (below, band))
    send_early(1)
    for d in range(2):
        far_copy(d).wait_recv()
        near_out[d, d] = (term[1 + d, d * part : (d + 1) * part] + far_in[d].astype(F32)).astype(BF16)
        near_copy(d, d).start()
    for n in range(2):
        near_copy(0, n).wait_recv()
        near_copy(1, n).wait_recv()
        own = term[3, n * part : (n + 1) * part]
        chi_ref[n * part : (n + 1) * part] = own + (near_in[0, n].astype(F32) + near_in[1, n].astype(F32))

    for index, ref in enumerate((pair, hop1, hop2)):
        remote(ref, ref, send_sem.at[index], w_sem.at[0], partner).wait_send()
    w_exchange.wait_send()
    for h in range(SIDE - 1):
        w_copy1(h).wait_send()
        w_copy2(h).wait_send()
    for sub in range(2):
        for d in range(2):
            halo_copy(d, sub).wait_send()
    for d in range(2):
        far_copy(d).wait_send()
        for n in range(2):
            near_copy(d, n).wait_send()


def reduce_partials(partial, det_taps, noise_var):
    smem = pl.BlockSpec(memory_space=pltpu.SMEM)
    vmem = pl.BlockSpec(memory_space=pltpu.VMEM)
    dma = pltpu.SemaphoreType.DMA
    height = PH // NBAND
    return pl.pallas_call(
        reduce_kernel,
        out_shape=(
            jax.ShapeDtypeStruct((PH, PH), F32),
            jax.ShapeDtypeStruct((height, PH), F32),
        ),
        in_specs=[vmem, smem, smem],
        out_specs=(vmem, vmem),
        scratch_shapes=[
            pltpu.VMEM((SLOTS, SIDE, SIDE, BLK, BLK), BF16),
            pltpu.VMEM((SLOTS, SIDE - 1, SIDE, BLK, BLK), BF16),
            pltpu.VMEM((SLOTS, SIDE - 1, BLK, BLK), BF16),
            pltpu.VMEM((2, SIDE, SIDE, 8, 128), F32),
            pltpu.VMEM((SIDE, SIDE, 8, 128), F32),
            pltpu.VMEM((2 * SIDE - 2, SIDE, 8, 128), F32),
            pltpu.VMEM((SIDE - 1, SIDE, 8, 128), F32),
            pltpu.VMEM((SIDE - 1, SIDE, 8, 128), F32),
            pltpu.VMEM((2, 2, 2, HALF, 128), BF16),
            pltpu.VMEM((2, 2, 2, HALF, 128), BF16),
            pltpu.VMEM((2, PH, PH), BF16),
            pltpu.VMEM((2, PH // 128, 128, PH), BF16),
            pltpu.VMEM((PH, PH), BF16),
            pltpu.VMEM((PH, PH), BF16),
            pltpu.VMEM((NBAND, height, PH), F32),
            pltpu.VMEM((2, height // 2, PH), BF16),
            pltpu.VMEM((2, height // 2, PH), BF16),
            pltpu.VMEM((2, 2, height // 2, PH), BF16),
            pltpu.VMEM((2, 2, height // 2, PH), BF16),
            dma((SLOTS, SIDE, SIDE)),
            dma((SLOTS, SIDE - 1, SIDE)),
            dma((SLOTS, SIDE - 1, 2)),
            dma((10,)),
            dma((7,)),
            dma((4,)),
            dma((2,)),
            dma((4,)),
            dma((10,)),
        ],
        compiler_params=pltpu.CompilerParams(
            vmem_limit_bytes=36 << 20, collective_id=0, has_side_effects=True
        ),
        name="reduce_partials",
    )(partial, det_taps, noise_var)


def write_kernel(image, chi, image_hbm, chi_hbm, sems):
    copies = [
        pltpu.make_async_copy(src, dst, sems.at[n]) for n, (src, dst) in enumerate(((image, image_hbm), (chi, chi_hbm)))
    ]
    for copy in copies:
        copy.start()
    for copy in copies:
        copy.wait()


def write_out(image, chi):
    hbm = pl.BlockSpec(memory_space=pltpu.HBM)
    vmem = pl.BlockSpec(memory_space=pltpu.VMEM)
    return pl.pallas_call(
        write_kernel,
        out_shape=tuple(jax.ShapeDtypeStruct(x.shape, x.dtype) for x in (image, chi)),
        in_specs=[vmem, vmem],
        out_specs=(hbm, hbm),
        scratch_shapes=[pltpu.SemaphoreType.DMA((2,))],
        name="write_out",
    )(*(pltpu.with_memory_space_constraint(x, pltpu.VMEM) for x in (image, chi)))


def local(blocks, dest_patch, dest_slot, weights, psf_taps, det_taps, noise_var):
    partial = match_partials(blocks, dest_patch, dest_slot, weights, psf_taps)
    partial = pltpu.with_memory_space_constraint(partial, pltpu.VMEM)
    image, chi = reduce_partials(partial, det_taps[0], noise_var)
    image, chi = write_out(image, chi)
    return image[None], chi


def solution(mesh):
    in_specs = (
        P("band", "patch", None, None),
        P("band", "patch"),
        P("band", "patch"),
        P("band", "patch"),
        P("band", "patch", None, None),
        P("band", None),
        P("band"),
    )
    out_specs = (P("band", None, "patch"), P("band", "patch"))
    return jax.shard_map(local, mesh=mesh, in_specs=in_specs, out_specs=out_specs, check_vma=False)
```

```python
import jax
import jax.numpy as jnp
from jax import lax
from jax.experimental import pallas as pl
from jax.experimental.pallas import tpu as pltpu
from jax.sharding import PartitionSpec as P

DR = 12
DTAPS = 25
SLOTS = 4
TAPS = 41
BLK = 256
HALF = 128
EDGE = 16
PH = 512
NPATCH = 32
NBAND = 4
SIDE = 4
GROUP = 4
STREAMS = ((1, 1), (1, -1), (0, 1), (0, -1))
BF16 = jnp.bfloat16
F32 = jnp.float32


def toeplitz_store(taps_row, matrix):
    rows = jnp.broadcast_to(taps_row, (16, 128))
    skew = pltpu.roll(rows, 0, 1, stride=1, stride_axis=0)
    zeros = jnp.zeros((16, 256), F32)
    wide = jnp.concatenate([zeros, skew, zeros], axis=1)
    for step in range(-9, 3):
        lo = 256 + 16 * step + 20
        tile = wide[:, lo : lo + 128].astype(BF16)
        rb = -step
        if rb >= 0:
            matrix[16 * rb : 16 * rb + 16, 0:128] = tile
        rb = 8 - step
        if rb < 16:
            matrix[16 * rb : 16 * rb + 16, 128:256] = tile


def match_kernel(
    patch_hbm, slot_hbm, weight_hbm, taps_hbm, blocks_hbm, out_ref,
    patch_ref, slot_ref, weight_ref, taps_ref, blocks, table_ref, tap_rows, weight_rows, even_mats, odd_mats, sems, small_sems,
):
    count = blocks.shape[0]

    def fetch(g):
        part = pl.ds(g * GROUP, GROUP)
        return pltpu.make_async_copy(blocks_hbm.at[0, part], blocks.at[part], sems.at[g])

    small = [
        pltpu.make_async_copy(src, dst, small_sems.at[n])
        for n, (src, dst) in enumerate(
            ((taps_hbm, taps_ref), (weight_hbm, weight_ref), (patch_hbm, patch_ref), (slot_hbm, slot_ref))
        )
    ]
    for copy in small:
        copy.start()
    for g in range(count // GROUP):
        fetch(g).start()
    even_mats[...] = jnp.zeros_like(even_mats)
    odd_mats[...] = jnp.zeros_like(odd_mats)
    table_ref[...] = jnp.zeros_like(table_ref)
    small[0].wait()
    raw = taps_ref[0].astype(F32).reshape(2 * count, TAPS).astype(BF16)
    from_tap = lax.broadcasted_iota(jnp.int32, (TAPS, 128), 0)
    to_lane = lax.broadcasted_iota(jnp.int32, (TAPS, 128), 1)
    for axis, picks in enumerate((from_tap == to_lane, from_tap + to_lane == TAPS - 1)):
        tap_rows[axis] = jnp.dot(raw, jnp.where(picks, 1.0, 0.0).astype(BF16), preferred_element_type=F32)
    groups = count // GROUP

    def build(g, mats):
        for n in range(GROUP):
            for axis in range(2):
                toeplitz_store(tap_rows[axis, pl.ds(2 * (g * GROUP + n) + axis, 1), :], mats.at[n, axis])

    build(0, even_mats)
    for copy in small[1:]:
        copy.wait()
    diagonal = lax.broadcasted_iota(jnp.int32, (count, count), 0) == lax.broadcasted_iota(jnp.int32, (count, count), 1)
    spread = jnp.where(diagonal, jnp.broadcast_to(weight_ref[...].astype(F32), (count, count)), 0.0)
    weight_rows[...] = jnp.broadcast_to(jnp.sum(spread, axis=1, keepdims=True), (count, 128))

    def match(g, mats, later):
        fetch(g).wait()
        build(lax.min(g + 1, groups - 1), later)
        halves = []
        for n in range(GROUP):
            half = jnp.dot(mats[n, 0], blocks[g * GROUP + n], preferred_element_type=F32)
            halves.append(half.astype(BF16))
        for n in range(GROUP):
            i = g * GROUP + n
            full = jnp.dot(halves[n], mats[n, 1], preferred_element_type=F32).astype(BF16)
            weight = weight_rows[pl.ds(i, 1), :]
            patch = patch_ref[0, i]
            slot = slot_ref[0, i]
            place = (patch & 1) * (SIDE * SIDE) + ((patch >> 1) & (SIDE - 1)) * SIDE + (patch >> 3)
            before = table_ref[place, pl.ds(slot, 1), :]
            table_ref[place, pl.ds(slot, 1), :] = before + weight
            wide = lambda row: jnp.broadcast_to(jnp.concatenate([row, row], axis=1), (BLK, BLK))
            tile = patch * SLOTS + slot
            old = jnp.where(wide(before) > 0.0, out_ref[tile].astype(F32), 0.0)
            out_ref[tile] = (old + wide(weight) * full.astype(F32)).astype(BF16)

    @pl.loop(0, groups // 2)
    def _(pair):
        match(2 * pair, even_mats, odd_mats)
        match(2 * pair + 1, odd_mats, even_mats)

    high, low = split(table_ref[...].reshape(NPATCH * 8, 128))
    out_ref[NPATCH * SLOTS, :, 0:128] = high
    out_ref[NPATCH * SLOTS, :, 128:256] = low


def match_partials(blocks, dest_patch, dest_slot, weights, taps):
    count = blocks.shape[1]
    hbm = pl.BlockSpec(memory_space=pltpu.HBM)
    vmem = pl.BlockSpec(memory_space=pltpu.VMEM)
    keep = lambda x: pltpu.with_memory_space_constraint(x, pltpu.HBM)
    return pl.pallas_call(
        match_kernel,
        out_shape=pltpu.VMEM((NPATCH * SLOTS + 1, BLK, BLK), BF16),
        in_specs=[hbm] * 5,
        out_specs=vmem,
        scratch_shapes=[
            pltpu.SMEM((1, count), jnp.int32),
            pltpu.SMEM((1, count), jnp.int32),
            pltpu.VMEM((1, count), BF16),
            pltpu.VMEM(taps.shape, BF16),
            pltpu.VMEM((count, BLK, BLK), BF16),
            pltpu.VMEM((NPATCH, 8, 128), F32),
            pltpu.VMEM((2, 2 * count, 128), F32),
            pltpu.VMEM((count, 128), F32),
            pltpu.VMEM((GROUP, 2, BLK, BLK), BF16),
            pltpu.VMEM((GROUP, 2, BLK, BLK), BF16),
            pltpu.SemaphoreType.DMA((count // GROUP,)),
            pltpu.SemaphoreType.DMA((4,)),
        ],
        compiler_params=pltpu.CompilerParams(vmem_limit_bytes=28 << 20),
        name="match_partials",
    )(*(keep(x) for x in (dest_patch, dest_slot, weights, taps, blocks)))


def wrap(x):
    return lax.rem(x + 2 * SIDE, SIDE)


def patch_index(y, z, core):
    return (y * SIDE + z) * 2 + core


def split(x):
    high = x.astype(BF16)
    return high, (x - high.astype(F32)).astype(BF16)


def dot3(ah, al, bh, bl):
    dot = lambda a, b: jnp.dot(a, b, preferred_element_type=F32)
    return dot(ah, bh) + (dot(ah, bl) + dot(al, bh))


def tap_block(det_ref, shift, sign):
    offset = lax.broadcasted_iota(jnp.int32, (128, 128), 1) - lax.broadcasted_iota(jnp.int32, (128, 128), 0)
    offset = sign * offset + shift + DR
    block = jnp.zeros((128, 128), F32)
    for t in range(DTAPS):
        block = jnp.where(offset == t, det_ref[t], block)
    return block


def build_tables(det_ref, col_tab, row_tab):
    col_tab[...] = jnp.zeros_like(col_tab)
    row_tab[...] = jnp.zeros_like(row_tab)
    for sign in (1, -1):
        for diag in (-1, 0, 1):
            high, low = split(tap_block(det_ref, sign * 128 * diag, sign))
            for rb in range(PH // 128):
                cb = rb + diag
                if 0 <= cb < PH // 128:
                    for n, part in enumerate((high, low)):
                        if sign == 1:
                            row_tab[n, rb, :, 128 * cb : 128 * cb + 128] = part
                        else:
                            col_tab[n, 128 * rb : 128 * rb + 128, 128 * cb : 128 * cb + 128] = part


def reduce_kernel(
    d_ref, det_ref, noise_ref, img_ref, chi_ref,
    pair, hop1, hop2, w_ref, w_pair, w_acc, w_hop1, w_hop2, halo_out, halo_in, col_tab, row_tab, high, low,
    term, far_out, far_in, near_out, near_in,
    pair_sem, hop1_sem, hop2_sem, send_sem, w_sem, halo_sem, far_sem, near_sem, end_sem,
):
    me = lax.axis_index("patch")
    band = lax.axis_index("band")
    core = lax.rem(me, 2)
    place = (lax.div(me, 2 * SIDE), lax.rem(lax.div(me, 2), SIDE))
    partner = me + 1 - 2 * core
    before = lax.rem(me + NPATCH - 1, NPATCH)
    after = lax.rem(me + 1, NPATCH)
    beside = lax.rem(me + NPATCH - 1 + 2 * core, NPATCH)

    def moved(axis, step):
        there = list(place)
        there[axis] = wrap(place[axis] + step)
        return patch_index(there[0], there[1], core)

    barrier = pltpu.get_barrier_semaphore()
    for device in (partner, beside, moved(0, 1), moved(0, -1), moved(1, 1), moved(1, -1)):
        pl.semaphore_signal(barrier, inc=1, device_id={"patch": device})
    above = lax.rem(band + 1, NBAND)
    below = lax.rem(band + NBAND - 1, NBAND)
    for device in (above, below):
        pl.semaphore_signal(barrier, inc=1, device_id={"band": device})
    pl.semaphore_wait(barrier, 8)

    def remote(src, dst, send, recv, device, axis="patch"):
        return pltpu.make_async_remote_copy(
            src_ref=src, dst_ref=dst, send_sem=send, recv_sem=recv, device_id={axis: device}
        )

    def dest(s, h, k):
        axis, step = STREAMS[s]
        first = wrap(place[axis] - step * (1 + h))
        other = wrap(place[1 - axis] - step * (1 + k))
        return (first, other) if axis == 0 else (other, first)

    def tile(s, h, k, parity):
        y, z = dest(s, h, k)
        return patch_index(y, z, parity) * SLOTS + s

    next1 = [moved(axis, step) for axis, step in STREAMS]
    next2 = [moved(1 - axis, step) for axis, step in STREAMS]

    def send_pair(s, h, k):
        remote(
            d_ref.at[tile(s, h, k, 1 - core)], pair.at[s, h, k], send_sem.at[0], pair_sem.at[s, h, k], partner
        ).start()

    def wait_pair(s, h, k):
        remote(pair.at[s, h, k], pair.at[s, h, k], send_sem.at[0], pair_sem.at[s, h, k], partner).wait_recv()

    def hop1_copy(s, h, k):
        return remote(pair.at[s, h, k], hop1.at[s, h, k], send_sem.at[1], hop1_sem.at[s, h, k], next1[s])

    def hop2_copy(s, k, sub):
        rows = pl.ds(sub * HALF, HALF)
        return remote(
            pair.at[s, 3, k, rows], hop2.at[s, k, rows], send_sem.at[2], hop2_sem.at[s, k, sub], next2[s]
        )

    table = d_ref[NPATCH * SLOTS]
    table = table[:, 0:128].astype(F32) + table[:, 128:256].astype(F32)
    w_ref[...] = table.reshape(2, SIDE, SIDE, 8, 128)
    w_exchange = remote(w_ref.at[1 - core], w_pair, send_sem.at[3], w_sem.at[0], partner)
    w_exchange.start()

    def send_pairs(h, first):
        @pl.loop(first, first + 2)
        def _(k):
            for s in range(SLOTS):
                send_pair(s, h, k)

    send_pairs(0, 0)
    w_exchange.wait_recv()

    def w_here(h):
        z = wrap(place[1] - 1 - h)
        return w_ref[core, z] + w_pair[z]

    def w_copy1(h):
        return remote(w_acc.at[h], w_hop1.at[h], send_sem.at[4 + h], w_sem.at[1 + h], moved(1, 1))

    def w_copy2(k):
        return remote(w_acc.at[3 + k], w_hop2.at[k], send_sem.at[7 + k], w_sem.at[4 + k], moved(0, 1))

    def here(s, h, k, rows=slice(0, BLK)):
        y, z = dest(s, h, k)
        height = rows.stop - rows.start
        wide = lambda row: jnp.broadcast_to(jnp.concatenate([row, row], axis=1), (height, BLK))
        mine = jnp.where(
            wide(w_ref[core, z, y, s : s + 1]) > 0.0, d_ref[tile(s, h, k, core), rows].astype(F32), 0.0
        )
        other = jnp.where(wide(w_pair[z, y, s : s + 1]) > 0.0, pair[s, h, k, rows].astype(F32), 0.0)
        return mine + other

    def start_units(first, *ahead):
        @pl.loop(first, first + 2)
        def _(k):
            for later, start in ahead:
                for s in range(SLOTS):
                    send_pair(s, later, k - first + start)
            for s in range(SLOTS):
                wait_pair(s, 0, k)
                pair[s, 0, k] = here(s, 0, k).astype(BF16)
                hop1_copy(s, 0, k).start()

    def pass_units(h, first, *ahead):
        @pl.loop(first, first + 2)
        def _(k):
            for later, start in ahead:
                for s in range(SLOTS):
                    send_pair(s, later, k - first + start)
            for s in range(SLOTS):
                wait_pair(s, h, k)
                total = here(s, h, k)
                hop1_copy(s, h - 1, k).wait_recv()
                pair[s, h, k] = (total + hop1[s, h - 1, k].astype(F32)).astype(BF16)
                hop1_copy(s, h, k).start()

    def gathered(s, k, sub):
        rows = slice(sub * HALF, (sub + 1) * HALF)
        if sub == 0:
            wait_pair(s, 3, k)
            hop1_copy(s, 2, k).wait_recv()
        total = here(s, 3, k, rows) + hop1[s, 2, k, rows].astype(F32)
        if k > 0:
            hop2_copy(s, k - 1, sub).wait_recv()
            total = total + hop2[s, k - 1, rows].astype(F32)
        return total

    def turn_units(k):
        for sub in range(2):
            for s in range(SLOTS):
                pair[s, 3, k, sub * HALF : (sub + 1) * HALF] = gathered(s, k, sub).astype(BF16)
                hop2_copy(s, k, sub).start()

    def w_step(n):
        if n > 0:
            (w_copy1(n - 1) if n < 4 else w_copy2(n - 4)).wait_recv()
        if n < 3:
            w_acc[n] = w_here(n) + w_hop1[n - 1] if n > 0 else w_here(n)
            w_copy1(n).start()
        else:
            w_acc[n] = w_here(3) + w_hop1[2] if n == 3 else w_acc[3] + w_hop2[n - 4]
            w_copy2(n - 3).start()

    w_step(0)
    start_units(0, (1, 0))
    build_tables(det_ref, col_tab, row_tab)
    pass_units(1, 0, (2, 0))
    w_step(1)
    pass_units(2, 0, (0, 2))
    w_step(2)
    start_units(2, (3, 0), (1, 2))
    w_step(3)
    turn_units(0)
    pass_units(1, 2, (2, 2))
    w_step(4)
    turn_units(1)
    pass_units(2, 2, (3, 2))
    w_step(5)
    turn_units(2)
    w_copy2(2).wait_recv()
    weight_sum = w_acc[3, place[0]] + w_hop2[2, place[0]]
    scale = 1.0 / jnp.maximum(weight_sum, 1.0)

    def halo_copy(d, sub):
        device = after if d == 0 else before
        return remote(
            halo_out.at[d, sub], halo_in.at[d, sub], end_sem.at[2 * sub + d], halo_sem.at[2 * sub + d], device
        )

    lane = lax.broadcasted_iota(jnp.int32, (EDGE, 128), 1) - lax.broadcasted_iota(jnp.int32, (EDGE, 128), 0)
    pick = [jnp.where(lane == first, 1.0, 0.0).astype(BF16) for first in (128 - EDGE, 0)]

    for sub in range(2):
        for s in range(SLOTS):
            value = gathered(s, 3, sub) * jnp.broadcast_to(scale[s : s + 1, 0:1], (HALF, BLK))
            top = (s // 2) * BLK + sub * HALF
            rows = slice(top, top + HALF)
            cols = slice((s % 2) * BLK, (s % 2 + 1) * BLK)
            img_ref[rows, cols] = value
            high[rows, cols], low[rows, cols] = split(value)
        tops = [half * BLK + sub * HALF for half in range(2)]
        for d, lane in enumerate((PH - 128, 0)):
            slab = jnp.concatenate([high[top : top + HALF, lane : lane + 128] for top in tops], axis=0)
            outermost = lax.dot_general(pick[d], slab, (((1,), (1,)), ((), ())), preferred_element_type=F32)
            halo_out[d, sub] = outermost.astype(BF16)
        for d in range(2):
            halo_copy(d, sub).start()

    high[...], low[...] = split(dot3(high[...], low[...], col_tab[0], col_tab[1]))
    height = PH // NBAND
    part = height // 2
    opposite = lax.rem(band + 2, NBAND)
    near = (above, below)
    over_noise = (1.0 / jnp.full((8, 128), noise_ref[0], F32))[0:1, 0:1]

    def row_tables(chunks):
        return [jnp.concatenate([row_tab[n, g] for g in chunks], axis=0) for n in range(2)]

    def rows_of(first, chunks, main=None):
        tables = row_tables(chunks)
        row = dot3(*tables, high[...], low[...]) if main is None else main
        edge = dot3(*tables, edge_high, edge_low)
        on_left = lax.broadcasted_iota(jnp.int32, edge.shape, 1) < 64
        row = jnp.concatenate(
            [
                row[:, 0:128] + jnp.where(on_left, edge, 0.0),
                row[:, 128 : PH - 128],
                row[:, PH - 128 : PH] + jnp.where(on_left, 0.0, edge),
            ],
            axis=1,
        )
        squares = row * row * jnp.broadcast_to(over_noise, row.shape)
        for n in range(len(chunks)):
            term[first + n] = squares[n * height : (n + 1) * height]

    far_copy = lambda d: remote(far_out.at[d], far_in.at[d], end_sem.at[4 + d], far_sem.at[d], near[d], "band")
    near_copy = lambda d, n: remote(
        near_out.at[d, n], near_in.at[d, n], end_sem.at[6 + 2 * d + n], near_sem.at[2 * d + n], near[d], "band"
    )

    def send_early(d):
        near_out[d, 1 - d] = term[1 + d, (1 - d) * part : (2 - d) * part].astype(BF16)
        near_copy(d, 1 - d).start()

    main = dot3(*row_tables((opposite,)), high[...], low[...])
    for sub in range(2):
        for d in range(2):
            halo_copy(d, sub).wait_recv()
    dot = lambda a, b: jnp.dot(a, b, preferred_element_type=F32)
    sides = [
        jnp.concatenate([halo_in[d, n % 2, :, n // 2 * HALF : n // 2 * HALF + HALF] for n in range(4)], axis=1)
        for d in range(2)
    ]
    gap = jnp.zeros((128 - EDGE, PH), BF16)
    sides = jnp.concatenate([gap, *sides, gap], axis=0)
    edge_turned = jnp.zeros((128, PH), F32)
    for n in range(2):
        corners = jnp.concatenate([row_tab[n, 1, :, 0:128], row_tab[n, 0, :, 128:256]], axis=1)
        edge_turned = edge_turned + jnp.dot(corners, sides, preferred_element_type=F32)
    edge_high, edge_low = split(edge_turned.T)
    rows_of(0, (opposite,), main)
    for d in range(2):
        far_out[d] = term[0, d * part : (d + 1) * part].astype(BF16)
        far_copy(d).start()
    rows_of(1, (above, below))
    send_early(0)
    send_early(1)
    rows_of(3, (band,))
    for d in range(2):
        far_copy(d).wait_recv()
        near_out[d, d] = (term[1 + d, d * part : (d + 1) * part] + far_in[d].astype(F32)).astype(BF16)
        near_copy(d, d).start()
    for n in range(2):
        near_copy(0, n).wait_recv()
        near_copy(1, n).wait_recv()
        own = term[3, n * part : (n + 1) * part]
        chi_ref[n * part : (n + 1) * part] = own + (near_in[0, n].astype(F32) + near_in[1, n].astype(F32))

    for index, ref in enumerate((pair, hop1, hop2)):
        remote(ref, ref, send_sem.at[index], w_sem.at[0], partner).wait_send()
    w_exchange.wait_send()
    for h in range(SIDE - 1):
        w_copy1(h).wait_send()
        w_copy2(h).wait_send()
    for sub in range(2):
        for d in range(2):
            halo_copy(d, sub).wait_send()
    for d in range(2):
        far_copy(d).wait_send()
        for n in range(2):
            near_copy(d, n).wait_send()


def reduce_partials(partial, det_taps, noise_var):
    smem = pl.BlockSpec(memory_space=pltpu.SMEM)
    vmem = pl.BlockSpec(memory_space=pltpu.VMEM)
    dma = pltpu.SemaphoreType.DMA
    height = PH // NBAND
    return pl.pallas_call(
        reduce_kernel,
        out_shape=(
            jax.ShapeDtypeStruct((PH, PH), F32),
            jax.ShapeDtypeStruct((height, PH), F32),
        ),
        in_specs=[vmem, smem, smem],
        out_specs=(vmem, vmem),
        scratch_shapes=[
            pltpu.VMEM((SLOTS, SIDE, SIDE, BLK, BLK), BF16),
            pltpu.VMEM((SLOTS, SIDE - 1, SIDE, BLK, BLK), BF16),
            pltpu.VMEM((SLOTS, SIDE - 1, BLK, BLK), BF16),
            pltpu.VMEM((2, SIDE, SIDE, 8, 128), F32),
            pltpu.VMEM((SIDE, SIDE, 8, 128), F32),
            pltpu.VMEM((2 * SIDE - 2, SIDE, 8, 128), F32),
            pltpu.VMEM((SIDE - 1, SIDE, 8, 128), F32),
            pltpu.VMEM((SIDE - 1, SIDE, 8, 128), F32),
            pltpu.VMEM((2, 2, EDGE, BLK), BF16),
            pltpu.VMEM((2, 2, EDGE, BLK), BF16),
            pltpu.VMEM((2, PH, PH), BF16),
            pltpu.VMEM((2, PH // 128, 128, PH), BF16),
            pltpu.VMEM((PH, PH), BF16),
            pltpu.VMEM((PH, PH), BF16),
            pltpu.VMEM((NBAND, height, PH), F32),
            pltpu.VMEM((2, height // 2, PH), BF16),
            pltpu.VMEM((2, height // 2, PH), BF16),
            pltpu.VMEM((2, 2, height // 2, PH), BF16),
            pltpu.VMEM((2, 2, height // 2, PH), BF16),
            dma((SLOTS, SIDE, SIDE)),
            dma((SLOTS, SIDE - 1, SIDE)),
            dma((SLOTS, SIDE - 1, 2)),
            dma((10,)),
            dma((7,)),
            dma((4,)),
            dma((2,)),
            dma((4,)),
            dma((10,)),
        ],
        compiler_params=pltpu.CompilerParams(
            vmem_limit_bytes=36 << 20, collective_id=0, has_side_effects=True
        ),
        name="reduce_partials",
    )(partial, det_taps, noise_var)


def write_kernel(image, chi, image_hbm, chi_hbm, sems):
    copies = [
        pltpu.make_async_copy(src, dst, sems.at[n]) for n, (src, dst) in enumerate(((image, image_hbm), (chi, chi_hbm)))
    ]
    for copy in copies:
        copy.start()
    for copy in copies:
        copy.wait()


def write_out(image, chi):
    hbm = pl.BlockSpec(memory_space=pltpu.HBM)
    vmem = pl.BlockSpec(memory_space=pltpu.VMEM)
    return pl.pallas_call(
        write_kernel,
        out_shape=tuple(jax.ShapeDtypeStruct(x.shape, x.dtype) for x in (image, chi)),
        in_specs=[vmem, vmem],
        out_specs=(hbm, hbm),
        scratch_shapes=[pltpu.SemaphoreType.DMA((2,))],
        name="write_out",
    )(*(pltpu.with_memory_space_constraint(x, pltpu.VMEM) for x in (image, chi)))


def local(blocks, dest_patch, dest_slot, weights, psf_taps, det_taps, noise_var):
    partial = match_partials(blocks, dest_patch, dest_slot, weights, psf_taps)
    partial = pltpu.with_memory_space_constraint(partial, pltpu.VMEM)
    image, chi = reduce_partials(partial, det_taps[0], noise_var)
    image, chi = write_out(image, chi)
    return image[None], chi


def solution(mesh):
    in_specs = (
        P("band", "patch", None, None),
        P("band", "patch"),
        P("band", "patch"),
        P("band", "patch"),
        P("band", "patch", None, None),
        P("band", None),
        P("band"),
    )
    out_specs = (P("band", None, "patch"), P("band", "patch"))
    return jax.shard_map(local, mesh=mesh, in_specs=in_specs, out_specs=out_specs, check_vma=False)
```

```python
import jax
import jax.numpy as jnp
from jax import lax
from jax.experimental import pallas as pl
from jax.experimental.pallas import tpu as pltpu
from jax.sharding import PartitionSpec as P

DR = 12
DTAPS = 25
SLOTS = 4
TAPS = 41
BLK = 256
HALF = 128
EDGE = 16
PH = 512
NPATCH = 32
NBAND = 4
SIDE = 4
GROUP = 4
STREAMS = ((1, 1), (1, -1), (0, 1), (0, -1))
BF16 = jnp.bfloat16
F32 = jnp.float32


def toeplitz_store(taps_row, matrix):
    rows = jnp.broadcast_to(taps_row, (16, 128))
    skew = pltpu.roll(rows, 0, 1, stride=1, stride_axis=0)
    zeros = jnp.zeros((16, 256), F32)
    wide = jnp.concatenate([zeros, skew, zeros], axis=1)
    for step in range(-9, 3):
        lo = 256 + 16 * step + 20
        tile = wide[:, lo : lo + 128].astype(BF16)
        rb = -step
        if rb >= 0:
            matrix[16 * rb : 16 * rb + 16, 0:128] = tile
        rb = 8 - step
        if rb < 16:
            matrix[16 * rb : 16 * rb + 16, 128:256] = tile


def match_kernel(
    patch_hbm, slot_hbm, weight_hbm, taps_hbm, blocks_hbm, out_ref,
    patch_ref, slot_ref, weight_ref, taps_ref, blocks, table_ref, tap_rows, weight_rows, even_mats, odd_mats, sems, small_sems,
):
    count = blocks.shape[0]

    def fetch(g):
        part = pl.ds(g * GROUP, GROUP)
        return pltpu.make_async_copy(blocks_hbm.at[0, part], blocks.at[part], sems.at[g])

    small = [
        pltpu.make_async_copy(src, dst, small_sems.at[n])
        for n, (src, dst) in enumerate(
            ((taps_hbm, taps_ref), (weight_hbm, weight_ref), (patch_hbm, patch_ref), (slot_hbm, slot_ref))
        )
    ]
    for copy in small:
        copy.start()
    for g in range(count // GROUP):
        fetch(g).start()
    even_mats[...] = jnp.zeros_like(even_mats)
    odd_mats[...] = jnp.zeros_like(odd_mats)
    table_ref[...] = jnp.zeros_like(table_ref)
    small[0].wait()
    raw = taps_ref[0].astype(F32).reshape(2 * count, TAPS).astype(BF16)
    from_tap = lax.broadcasted_iota(jnp.int32, (TAPS, 128), 0)
    to_lane = lax.broadcasted_iota(jnp.int32, (TAPS, 128), 1)
    for axis, picks in enumerate((from_tap == to_lane, from_tap + to_lane == TAPS - 1)):
        tap_rows[axis] = jnp.dot(raw, jnp.where(picks, 1.0, 0.0).astype(BF16), preferred_element_type=F32)
    groups = count // GROUP

    def build(g, mats):
        for n in range(GROUP):
            for axis in range(2):
                toeplitz_store(tap_rows[axis, pl.ds(2 * (g * GROUP + n) + axis, 1), :], mats.at[n, axis])

    build(0, even_mats)
    for copy in small[1:]:
        copy.wait()
    diagonal = lax.broadcasted_iota(jnp.int32, (count, count), 0) == lax.broadcasted_iota(jnp.int32, (count, count), 1)
    spread = jnp.where(diagonal, jnp.broadcast_to(weight_ref[...].astype(F32), (count, count)), 0.0)
    weight_rows[...] = jnp.broadcast_to(jnp.sum(spread, axis=1, keepdims=True), (count, 128))

    def match(g, mats, later):
        fetch(g).wait()
        build(lax.min(g + 1, groups - 1), later)
        halves = []
        for n in range(GROUP):
            half = jnp.dot(mats[n, 0], blocks[g * GROUP + n], preferred_element_type=F32)
            halves.append(half.astype(BF16))
        for n in range(GROUP):
            i = g * GROUP + n
            full = jnp.dot(halves[n], mats[n, 1], preferred_element_type=F32).astype(BF16)
            weight = weight_rows[pl.ds(i, 1), :]
            patch = patch_ref[0, i]
            slot = slot_ref[0, i]
            place = (patch & 1) * (SIDE * SIDE) + ((patch >> 1) & (SIDE - 1)) * SIDE + (patch >> 3)
            before = table_ref[place, pl.ds(slot, 1), :]
            table_ref[place, pl.ds(slot, 1), :] = before + weight
            wide = lambda row: jnp.broadcast_to(jnp.concatenate([row, row], axis=1), (BLK, BLK))
            tile = patch * SLOTS + slot
            old = jnp.where(wide(before) > 0.0, out_ref[tile].astype(F32), 0.0)
            out_ref[tile] = (old + wide(weight) * full.astype(F32)).astype(BF16)

    @pl.loop(0, groups // 2)
    def _(pair):
        match(2 * pair, even_mats, odd_mats)
        match(2 * pair + 1, odd_mats, even_mats)

    high, low = split(table_ref[...].reshape(NPATCH * 8, 128))
    out_ref[NPATCH * SLOTS, :, 0:128] = high
    out_ref[NPATCH * SLOTS, :, 128:256] = low


def match_partials(blocks, dest_patch, dest_slot, weights, taps):
    count = blocks.shape[1]
    hbm = pl.BlockSpec(memory_space=pltpu.HBM)
    vmem = pl.BlockSpec(memory_space=pltpu.VMEM)
    keep = lambda x: pltpu.with_memory_space_constraint(x, pltpu.HBM)
    return pl.pallas_call(
        match_kernel,
        out_shape=pltpu.VMEM((NPATCH * SLOTS + 1, BLK, BLK), BF16),
        in_specs=[hbm] * 5,
        out_specs=vmem,
        scratch_shapes=[
            pltpu.SMEM((1, count), jnp.int32),
            pltpu.SMEM((1, count), jnp.int32),
            pltpu.VMEM((1, count), BF16),
            pltpu.VMEM(taps.shape, BF16),
            pltpu.VMEM((count, BLK, BLK), BF16),
            pltpu.VMEM((NPATCH, 8, 128), F32),
            pltpu.VMEM((2, 2 * count, 128), F32),
            pltpu.VMEM((count, 128), F32),
            pltpu.VMEM((GROUP, 2, BLK, BLK), BF16),
            pltpu.VMEM((GROUP, 2, BLK, BLK), BF16),
            pltpu.SemaphoreType.DMA((count // GROUP,)),
            pltpu.SemaphoreType.DMA((4,)),
        ],
        compiler_params=pltpu.CompilerParams(vmem_limit_bytes=28 << 20),
        name="match_partials",
    )(*(keep(x) for x in (dest_patch, dest_slot, weights, taps, blocks)))


def wrap(x):
    return lax.rem(x + 2 * SIDE, SIDE)


def patch_index(y, z, core):
    return (y * SIDE + z) * 2 + core


def split(x):
    high = x.astype(BF16)
    return high, (x - high.astype(F32)).astype(BF16)


def dot3(ah, al, bh, bl):
    dot = lambda a, b: jnp.dot(a, b, preferred_element_type=F32)
    return dot(ah, bh) + (dot(ah, bl) + dot(al, bh))


def tap_block(det_ref, shift, sign):
    offset = lax.broadcasted_iota(jnp.int32, (128, 128), 1) - lax.broadcasted_iota(jnp.int32, (128, 128), 0)
    offset = sign * offset + shift + DR
    block = jnp.zeros((128, 128), F32)
    for t in range(DTAPS):
        block = jnp.where(offset == t, det_ref[0, t], block)
    return block


def build_tables(det_ref, col_tab, row_tab):
    col_tab[...] = jnp.zeros_like(col_tab)
    row_tab[...] = jnp.zeros_like(row_tab)
    for sign in (1, -1):
        for diag in (-1, 0, 1):
            high, low = split(tap_block(det_ref, sign * 128 * diag, sign))
            for rb in range(PH // 128):
                cb = rb + diag
                if 0 <= cb < PH // 128:
                    for n, part in enumerate((high, low)):
                        if sign == 1:
                            row_tab[n, rb, :, 128 * cb : 128 * cb + 128] = part
                        else:
                            col_tab[n, 128 * rb : 128 * rb + 128, 128 * cb : 128 * cb + 128] = part


def reduce_kernel(
    d_ref, det_hbm, noise_ref, img_ref, chi_ref,
    det_ref,    pair, hop1, hop2, w_ref, w_pair, w_acc, w_hop1, w_hop2, halo_out, halo_in, col_tab, row_tab, high, low,
    term, far_out, far_in, near_out, near_in,
    pair_sem, hop1_sem, hop2_sem, send_sem, w_sem, halo_sem, far_sem, near_sem, end_sem, small_sem,
):
    taps_copy = pltpu.make_async_copy(det_hbm, det_ref, small_sem.at[0])
    taps_copy.start()
    me = lax.axis_index("patch")
    band = lax.axis_index("band")
    core = lax.rem(me, 2)
    place = (lax.div(me, 2 * SIDE), lax.rem(lax.div(me, 2), SIDE))
    partner = me + 1 - 2 * core
    before = lax.rem(me + NPATCH - 1, NPATCH)
    after = lax.rem(me + 1, NPATCH)
    beside = lax.rem(me + NPATCH - 1 + 2 * core, NPATCH)

    def moved(axis, step):
        there = list(place)
        there[axis] = wrap(place[axis] + step)
        return patch_index(there[0], there[1], core)

    barrier = pltpu.get_barrier_semaphore()
    for device in (partner, beside, moved(0, 1), moved(0, -1), moved(1, 1), moved(1, -1)):
        pl.semaphore_signal(barrier, inc=1, device_id={"patch": device})
    above = lax.rem(band + 1, NBAND)
    below = lax.rem(band + NBAND - 1, NBAND)
    for device in (above, below):
        pl.semaphore_signal(barrier, inc=1, device_id={"band": device})
    pl.semaphore_wait(barrier, 8)

    def remote(src, dst, send, recv, device, axis="patch"):
        return pltpu.make_async_remote_copy(
            src_ref=src, dst_ref=dst, send_sem=send, recv_sem=recv, device_id={axis: device}
        )

    def dest(s, h, k):
        axis, step = STREAMS[s]
        first = wrap(place[axis] - step * (1 + h))
        other = wrap(place[1 - axis] - step * (1 + k))
        return (first, other) if axis == 0 else (other, first)

    def tile(s, h, k, parity):
        y, z = dest(s, h, k)
        return patch_index(y, z, parity) * SLOTS + s

    next1 = [moved(axis, step) for axis, step in STREAMS]
    next2 = [moved(1 - axis, step) for axis, step in STREAMS]

    def send_pair(s, h, k):
        remote(
            d_ref.at[tile(s, h, k, 1 - core)], pair.at[s, h, k], send_sem.at[0], pair_sem.at[s, h, k], partner
        ).start()

    def wait_pair(s, h, k):
        remote(pair.at[s, h, k], pair.at[s, h, k], send_sem.at[0], pair_sem.at[s, h, k], partner).wait_recv()

    def hop1_copy(s, h, k):
        return remote(pair.at[s, h, k], hop1.at[s, h, k], send_sem.at[1], hop1_sem.at[s, h, k], next1[s])

    def hop2_copy(s, k, sub):
        rows = pl.ds(sub * HALF, HALF)
        return remote(
            pair.at[s, 3, k, rows], hop2.at[s, k, rows], send_sem.at[2], hop2_sem.at[s, k, sub], next2[s]
        )

    table = d_ref[NPATCH * SLOTS]
    table = table[:, 0:128].astype(F32) + table[:, 128:256].astype(F32)
    w_ref[...] = table.reshape(2, SIDE, SIDE, 8, 128)
    w_exchange = remote(w_ref.at[1 - core], w_pair, send_sem.at[3], w_sem.at[0], partner)
    w_exchange.start()

    def send_pairs(h, first):
        @pl.loop(first, first + 2)
        def _(k):
            for s in range(SLOTS):
                send_pair(s, h, k)

    send_pairs(0, 0)
    w_exchange.wait_recv()

    def w_here(h):
        z = wrap(place[1] - 1 - h)
        return w_ref[core, z] + w_pair[z]

    def w_copy1(h):
        return remote(w_acc.at[h], w_hop1.at[h], send_sem.at[4 + h], w_sem.at[1 + h], moved(1, 1))

    def w_copy2(k):
        return remote(w_acc.at[3 + k], w_hop2.at[k], send_sem.at[7 + k], w_sem.at[4 + k], moved(0, 1))

    def here(s, h, k, rows=slice(0, BLK)):
        y, z = dest(s, h, k)
        height = rows.stop - rows.start
        wide = lambda row: jnp.broadcast_to(jnp.concatenate([row, row], axis=1), (height, BLK))
        mine = jnp.where(
            wide(w_ref[core, z, y, s : s + 1]) > 0.0, d_ref[tile(s, h, k, core), rows].astype(F32), 0.0
        )
        other = jnp.where(wide(w_pair[z, y, s : s + 1]) > 0.0, pair[s, h, k, rows].astype(F32), 0.0)
        return mine + other

    def start_units(first, *ahead):
        @pl.loop(first, first + 2)
        def _(k):
            for later, start in ahead:
                for s in range(SLOTS):
                    send_pair(s, later, k - first + start)
            for s in range(SLOTS):
                wait_pair(s, 0, k)
                pair[s, 0, k] = here(s, 0, k).astype(BF16)
                hop1_copy(s, 0, k).start()

    def pass_units(h, first, *ahead):
        @pl.loop(first, first + 2)
        def _(k):
            for later, start in ahead:
                for s in range(SLOTS):
                    send_pair(s, later, k - first + start)
            for s in range(SLOTS):
                wait_pair(s, h, k)
                total = here(s, h, k)
                hop1_copy(s, h - 1, k).wait_recv()
                pair[s, h, k] = (total + hop1[s, h - 1, k].astype(F32)).astype(BF16)
                hop1_copy(s, h, k).start()

    def gathered(s, k, sub):
        rows = slice(sub * HALF, (sub + 1) * HALF)
        if sub == 0:
            wait_pair(s, 3, k)
            hop1_copy(s, 2, k).wait_recv()
        total = here(s, 3, k, rows) + hop1[s, 2, k, rows].astype(F32)
        if k > 0:
            hop2_copy(s, k - 1, sub).wait_recv()
            total = total + hop2[s, k - 1, rows].astype(F32)
        return total

    def turn_units(k):
        for sub in range(2):
            for s in range(SLOTS):
                pair[s, 3, k, sub * HALF : (sub + 1) * HALF] = gathered(s, k, sub).astype(BF16)
                hop2_copy(s, k, sub).start()

    def w_step(n):
        if n > 0:
            (w_copy1(n - 1) if n < 4 else w_copy2(n - 4)).wait_recv()
        if n < 3:
            w_acc[n] = w_here(n) + w_hop1[n - 1] if n > 0 else w_here(n)
            w_copy1(n).start()
        else:
            w_acc[n] = w_here(3) + w_hop1[2] if n == 3 else w_acc[3] + w_hop2[n - 4]
            w_copy2(n - 3).start()

    w_step(0)
    start_units(0, (1, 0))
    taps_copy.wait()
    build_tables(det_ref, col_tab, row_tab)
    pass_units(1, 0, (2, 0))
    w_step(1)
    pass_units(2, 0, (0, 2))
    w_step(2)
    start_units(2, (3, 0), (1, 2))
    w_step(3)
    turn_units(0)
    pass_units(1, 2, (2, 2))
    w_step(4)
    turn_units(1)
    pass_units(2, 2, (3, 2))
    w_step(5)
    turn_units(2)
    w_copy2(2).wait_recv()
    weight_sum = w_acc[3, place[0]] + w_hop2[2, place[0]]
    scale = 1.0 / jnp.maximum(weight_sum, 1.0)

    def halo_copy(d, sub):
        device = after if d == 0 else before
        return remote(
            halo_out.at[d, sub], halo_in.at[d, sub], end_sem.at[2 * sub + d], halo_sem.at[2 * sub + d], device
        )

    lane = lax.broadcasted_iota(jnp.int32, (EDGE, 128), 1) - lax.broadcasted_iota(jnp.int32, (EDGE, 128), 0)
    pick = [jnp.where(lane == first, 1.0, 0.0).astype(BF16) for first in (128 - EDGE, 0)]

    for sub in range(2):
        for s in range(SLOTS):
            value = gathered(s, 3, sub) * jnp.broadcast_to(scale[s : s + 1, 0:1], (HALF, BLK))
            top = (s // 2) * BLK + sub * HALF
            rows = slice(top, top + HALF)
            cols = slice((s % 2) * BLK, (s % 2 + 1) * BLK)
            img_ref[rows, cols] = value
            high[rows, cols], low[rows, cols] = split(value)
        tops = [half * BLK + sub * HALF for half in range(2)]
        for d, lane in enumerate((PH - 128, 0)):
            slab = jnp.concatenate([high[top : top + HALF, lane : lane + 128] for top in tops], axis=0)
            outermost = lax.dot_general(pick[d], slab, (((1,), (1,)), ((), ())), preferred_element_type=F32)
            halo_out[d, sub] = outermost.astype(BF16)
        for d in range(2):
            halo_copy(d, sub).start()

    high[...], low[...] = split(dot3(high[...], low[...], col_tab[0], col_tab[1]))
    height = PH // NBAND
    part = height // 2
    opposite = lax.rem(band + 2, NBAND)
    near = (above, below)
    over_noise = 1.0 / noise_ref[...]

    def row_tables(chunks):
        return [jnp.concatenate([row_tab[n, g] for g in chunks], axis=0) for n in range(2)]

    def rows_of(first, chunks, main=None):
        tables = row_tables(chunks)
        row = dot3(*tables, high[...], low[...]) if main is None else main
        edge = dot3(*tables, edge_high, edge_low)
        on_left = lax.broadcasted_iota(jnp.int32, edge.shape, 1) < 64
        row = jnp.concatenate(
            [
                row[:, 0:128] + jnp.where(on_left, edge, 0.0),
                row[:, 128 : PH - 128],
                row[:, PH - 128 : PH] + jnp.where(on_left, 0.0, edge),
            ],
            axis=1,
        )
        squares = row * row * jnp.broadcast_to(over_noise, row.shape)
        for n in range(len(chunks)):
            term[first + n] = squares[n * height : (n + 1) * height]

    far_copy = lambda d: remote(far_out.at[d], far_in.at[d], end_sem.at[4 + d], far_sem.at[d], near[d], "band")
    near_copy = lambda d, n: remote(
        near_out.at[d, n], near_in.at[d, n], end_sem.at[6 + 2 * d + n], near_sem.at[2 * d + n], near[d], "band"
    )

    def send_early(d):
        near_out[d, 1 - d] = term[1 + d, (1 - d) * part : (2 - d) * part].astype(BF16)
        near_copy(d, 1 - d).start()

    main = dot3(*row_tables((opposite,)), high[...], low[...])
    for sub in range(2):
        for d in range(2):
            halo_copy(d, sub).wait_recv()
    dot = lambda a, b: jnp.dot(a, b, preferred_element_type=F32)
    sides = [
        jnp.concatenate([halo_in[d, n % 2, :, n // 2 * HALF : n // 2 * HALF + HALF] for n in range(4)], axis=1)
        for d in range(2)
    ]
    gap = jnp.zeros((128 - EDGE, PH), BF16)
    sides = jnp.concatenate([gap, *sides, gap], axis=0)
    edge_turned = jnp.zeros((128, PH), F32)
    for n in range(2):
        corners = jnp.concatenate([row_tab[n, 1, :, 0:128], row_tab[n, 0, :, 128:256]], axis=1)
        edge_turned = edge_turned + jnp.dot(corners, sides, preferred_element_type=F32)
    edge_high, edge_low = split(edge_turned.T)
    rows_of(0, (opposite,), main)
    for d in range(2):
        far_out[d] = term[0, d * part : (d + 1) * part].astype(BF16)
        far_copy(d).start()
    rows_of(1, (above, below))
    send_early(0)
    send_early(1)
    rows_of(3, (band,))
    for d in range(2):
        far_copy(d).wait_recv()
        near_out[d, d] = (term[1 + d, d * part : (d + 1) * part] + far_in[d].astype(F32)).astype(BF16)
        near_copy(d, d).start()
    for n in range(2):
        near_copy(0, n).wait_recv()
        near_copy(1, n).wait_recv()
        own = term[3, n * part : (n + 1) * part]
        chi_ref[n * part : (n + 1) * part] = own + (near_in[0, n].astype(F32) + near_in[1, n].astype(F32))

    for index, ref in enumerate((pair, hop1, hop2)):
        remote(ref, ref, send_sem.at[index], w_sem.at[0], partner).wait_send()
    w_exchange.wait_send()
    for h in range(SIDE - 1):
        w_copy1(h).wait_send()
        w_copy2(h).wait_send()
    for sub in range(2):
        for d in range(2):
            halo_copy(d, sub).wait_send()
    for d in range(2):
        far_copy(d).wait_send()
        for n in range(2):
            near_copy(d, n).wait_send()


def reduce_partials(partial, det_taps, noise_var):
    hbm = pl.BlockSpec(memory_space=pltpu.HBM)
    keep = lambda x: pltpu.with_memory_space_constraint(x, pltpu.HBM)
    vmem = pl.BlockSpec(memory_space=pltpu.VMEM)
    dma = pltpu.SemaphoreType.DMA
    height = PH // NBAND
    return pl.pallas_call(
        reduce_kernel,
        out_shape=(
            jax.ShapeDtypeStruct((PH, PH), F32),
            jax.ShapeDtypeStruct((height, PH), F32),
        ),
        in_specs=[vmem, hbm, vmem],
        out_specs=(vmem, vmem),
        scratch_shapes=[
            pltpu.SMEM(det_taps.shape, F32),
            pltpu.VMEM((SLOTS, SIDE, SIDE, BLK, BLK), BF16),
            pltpu.VMEM((SLOTS, SIDE - 1, SIDE, BLK, BLK), BF16),
            pltpu.VMEM((SLOTS, SIDE - 1, BLK, BLK), BF16),
            pltpu.VMEM((2, SIDE, SIDE, 8, 128), F32),
            pltpu.VMEM((SIDE, SIDE, 8, 128), F32),
            pltpu.VMEM((2 * SIDE - 2, SIDE, 8, 128), F32),
            pltpu.VMEM((SIDE - 1, SIDE, 8, 128), F32),
            pltpu.VMEM((SIDE - 1, SIDE, 8, 128), F32),
            pltpu.VMEM((2, 2, EDGE, BLK), BF16),
            pltpu.VMEM((2, 2, EDGE, BLK), BF16),
            pltpu.VMEM((2, PH, PH), BF16),
            pltpu.VMEM((2, PH // 128, 128, PH), BF16),
            pltpu.VMEM((PH, PH), BF16),
            pltpu.VMEM((PH, PH), BF16),
            pltpu.VMEM((NBAND, height, PH), F32),
            pltpu.VMEM((2, height // 2, PH), BF16),
            pltpu.VMEM((2, height // 2, PH), BF16),
            pltpu.VMEM((2, 2, height // 2, PH), BF16),
            pltpu.VMEM((2, 2, height // 2, PH), BF16),
            dma((SLOTS, SIDE, SIDE)),
            dma((SLOTS, SIDE - 1, SIDE)),
            dma((SLOTS, SIDE - 1, 2)),
            dma((10,)),
            dma((7,)),
            dma((4,)),
            dma((2,)),
            dma((4,)),
            dma((10,)),
            dma((1,)),
        ],
        compiler_params=pltpu.CompilerParams(
            vmem_limit_bytes=36 << 20, collective_id=0, has_side_effects=True
        ),
        name="reduce_partials",
    )(partial, keep(det_taps), noise_var)


def write_kernel(image, chi, image_hbm, chi_hbm, sems):
    copies = [
        pltpu.make_async_copy(src, dst, sems.at[n]) for n, (src, dst) in enumerate(((image, image_hbm), (chi, chi_hbm)))
    ]
    for copy in copies:
        copy.start()
    for copy in copies:
        copy.wait()


def write_out(image, chi):
    hbm = pl.BlockSpec(memory_space=pltpu.HBM)
    vmem = pl.BlockSpec(memory_space=pltpu.VMEM)
    return pl.pallas_call(
        write_kernel,
        out_shape=tuple(jax.ShapeDtypeStruct(x.shape, x.dtype) for x in (image, chi)),
        in_specs=[vmem, vmem],
        out_specs=(hbm, hbm),
        scratch_shapes=[pltpu.SemaphoreType.DMA((2,))],
        name="write_out",
    )(*(pltpu.with_memory_space_constraint(x, pltpu.VMEM) for x in (image, chi)))


def local(blocks, dest_patch, dest_slot, weights, psf_taps, det_taps, noise_var):
    partial = match_partials(blocks, dest_patch, dest_slot, weights, psf_taps)
    partial = pltpu.with_memory_space_constraint(partial, pltpu.VMEM)
    image, chi = reduce_partials(partial, det_taps, noise_var.reshape(1, 1))
    image, chi = write_out(image, chi)
    return image[None], chi


def solution(mesh):
    in_specs = (
        P("band", "patch", None, None),
        P("band", "patch"),
        P("band", "patch"),
        P("band", "patch"),
        P("band", "patch", None, None),
        P("band", None),
        P("band"),
    )
    out_specs = (P("band", None, "patch"), P("band", "patch"))
    return jax.shard_map(local, mesh=mesh, in_specs=in_specs, out_specs=out_specs, check_vma=False)
```

```python
import jax
import jax.numpy as jnp
from jax import lax
from jax.experimental import pallas as pl
from jax.experimental.pallas import tpu as pltpu
from jax.sharding import PartitionSpec as P

DR = 12
DTAPS = 25
SLOTS = 4
TAPS = 41
BLK = 256
HALF = 128
EDGE = 16
PH = 512
NPATCH = 32
NBAND = 4
SIDE = 4
GROUP = 4
STREAMS = ((1, 1), (1, -1), (0, 1), (0, -1))
BF16 = jnp.bfloat16
F32 = jnp.float32


def toeplitz_store(taps_row, matrix):
    rows = jnp.broadcast_to(taps_row, (16, 128))
    skew = pltpu.roll(rows, 0, 1, stride=1, stride_axis=0)
    zeros = jnp.zeros((16, 256), F32)
    wide = jnp.concatenate([zeros, skew, zeros], axis=1)
    for step in range(-9, 3):
        lo = 256 + 16 * step + 20
        tile = wide[:, lo : lo + 128].astype(BF16)
        rb = -step
        if rb >= 0:
            matrix[16 * rb : 16 * rb + 16, 0:128] = tile
        rb = 8 - step
        if rb < 16:
            matrix[16 * rb : 16 * rb + 16, 128:256] = tile


def match_kernel(
    patch_hbm, slot_hbm, weight_hbm, taps_hbm, blocks_hbm, out_ref,
    patch_ref, slot_ref, weight_ref, taps_ref, blocks, table_ref, tap_rows, weight_rows, even_mats, odd_mats, sems, small_sems,
):
    count = blocks.shape[0]

    def fetch(g):
        part = pl.ds(g * GROUP, GROUP)
        return pltpu.make_async_copy(blocks_hbm.at[0, part], blocks.at[part], sems.at[g])

    small = [
        pltpu.make_async_copy(src, dst, small_sems.at[n])
        for n, (src, dst) in enumerate(
            ((taps_hbm, taps_ref), (weight_hbm, weight_ref), (patch_hbm, patch_ref), (slot_hbm, slot_ref))
        )
    ]
    small[0].start()
    fetch(0).start()
    for copy in small[1:]:
        copy.start()
    for g in range(1, count // GROUP):
        fetch(g).start()
    even_mats[...] = jnp.zeros_like(even_mats)
    odd_mats[...] = jnp.zeros_like(odd_mats)
    table_ref[...] = jnp.zeros_like(table_ref)
    small[0].wait()
    raw = taps_ref[0].astype(F32).reshape(2 * count, TAPS).astype(BF16)
    from_tap = lax.broadcasted_iota(jnp.int32, (TAPS, 128), 0)
    to_lane = lax.broadcasted_iota(jnp.int32, (TAPS, 128), 1)
    for axis, picks in enumerate((from_tap == to_lane, from_tap + to_lane == TAPS - 1)):
        tap_rows[axis] = jnp.dot(raw, jnp.where(picks, 1.0, 0.0).astype(BF16), preferred_element_type=F32)
    groups = count // GROUP

    def build(g, mats):
        for n in range(GROUP):
            for axis in range(2):
                toeplitz_store(tap_rows[axis, pl.ds(2 * (g * GROUP + n) + axis, 1), :], mats.at[n, axis])

    build(0, even_mats)
    for copy in small[1:]:
        copy.wait()
    diagonal = lax.broadcasted_iota(jnp.int32, (count, count), 0) == lax.broadcasted_iota(jnp.int32, (count, count), 1)
    spread = jnp.where(diagonal, jnp.broadcast_to(weight_ref[...].astype(F32), (count, count)), 0.0)
    weight_rows[...] = jnp.broadcast_to(jnp.sum(spread, axis=1, keepdims=True), (count, 128))

    def match(g, mats, later):
        fetch(g).wait()
        build(lax.min(g + 1, groups - 1), later)
        halves = []
        for n in range(GROUP):
            half = jnp.dot(mats[n, 0], blocks[g * GROUP + n], preferred_element_type=F32)
            halves.append(half.astype(BF16))
        for n in range(GROUP):
            i = g * GROUP + n
            full = jnp.dot(halves[n], mats[n, 1], preferred_element_type=F32).astype(BF16)
            weight = weight_rows[pl.ds(i, 1), :]
            patch = patch_ref[0, i]
            slot = slot_ref[0, i]
            place = (patch & 1) * (SIDE * SIDE) + ((patch >> 1) & (SIDE - 1)) * SIDE + (patch >> 3)
            before = table_ref[place, pl.ds(slot, 1), :]
            table_ref[place, pl.ds(slot, 1), :] = before + weight
            wide = lambda row: jnp.broadcast_to(jnp.concatenate([row, row], axis=1), (BLK, BLK))
            tile = patch * SLOTS + slot
            old = jnp.where(wide(before) > 0.0, out_ref[tile].astype(F32), 0.0)
            out_ref[tile] = (old + wide(weight) * full.astype(F32)).astype(BF16)

    @pl.loop(0, groups // 2)
    def _(pair):
        match(2 * pair, even_mats, odd_mats)
        match(2 * pair + 1, odd_mats, even_mats)

    high, low = split(table_ref[...].reshape(NPATCH * 8, 128))
    out_ref[NPATCH * SLOTS, :, 0:128] = high
    out_ref[NPATCH * SLOTS, :, 128:256] = low


def match_partials(blocks, dest_patch, dest_slot, weights, taps):
    count = blocks.shape[1]
    hbm = pl.BlockSpec(memory_space=pltpu.HBM)
    vmem = pl.BlockSpec(memory_space=pltpu.VMEM)
    keep = lambda x: pltpu.with_memory_space_constraint(x, pltpu.HBM)
    return pl.pallas_call(
        match_kernel,
        out_shape=pltpu.VMEM((NPATCH * SLOTS + 1, BLK, BLK), BF16),
        in_specs=[hbm] * 5,
        out_specs=vmem,
        scratch_shapes=[
            pltpu.SMEM((1, count), jnp.int32),
            pltpu.SMEM((1, count), jnp.int32),
            pltpu.VMEM((1, count), BF16),
            pltpu.VMEM(taps.shape, BF16),
            pltpu.VMEM((count, BLK, BLK), BF16),
            pltpu.VMEM((NPATCH, 8, 128), F32),
            pltpu.VMEM((2, 2 * count, 128), F32),
            pltpu.VMEM((count, 128), F32),
            pltpu.VMEM((GROUP, 2, BLK, BLK), BF16),
            pltpu.VMEM((GROUP, 2, BLK, BLK), BF16),
            pltpu.SemaphoreType.DMA((count // GROUP,)),
            pltpu.SemaphoreType.DMA((4,)),
        ],
        compiler_params=pltpu.CompilerParams(vmem_limit_bytes=28 << 20),
        name="match_partials",
    )(*(keep(x) for x in (dest_patch, dest_slot, weights, taps, blocks)))


def wrap(x):
    return lax.rem(x + 2 * SIDE, SIDE)


def patch_index(y, z, core):
    return (y * SIDE + z) * 2 + core


def split(x):
    high = x.astype(BF16)
    return high, (x - high.astype(F32)).astype(BF16)


def dot3(ah, al, bh, bl):
    dot = lambda a, b: jnp.dot(a, b, preferred_element_type=F32)
    return dot(ah, bh) + (dot(ah, bl) + dot(al, bh))


def tap_block(det_ref, shift, sign):
    offset = lax.broadcasted_iota(jnp.int32, (128, 128), 1) - lax.broadcasted_iota(jnp.int32, (128, 128), 0)
    offset = sign * offset + shift + DR
    block = jnp.zeros((128, 128), F32)
    for t in range(DTAPS):
        block = jnp.where(offset == t, det_ref[0, t], block)
    return block


def build_tables(det_ref, col_tab, row_tab):
    col_tab[...] = jnp.zeros_like(col_tab)
    row_tab[...] = jnp.zeros_like(row_tab)
    for sign in (1, -1):
        for diag in (-1, 0, 1):
            high, low = split(tap_block(det_ref, sign * 128 * diag, sign))
            for rb in range(PH // 128):
                cb = rb + diag
                if 0 <= cb < PH // 128:
                    for n, part in enumerate((high, low)):
                        if sign == 1:
                            row_tab[n, rb, :, 128 * cb : 128 * cb + 128] = part
                        else:
                            col_tab[n, 128 * rb : 128 * rb + 128, 128 * cb : 128 * cb + 128] = part


def reduce_kernel(
    d_ref, det_hbm, noise_ref, img_ref, chi_ref,
    det_ref,    pair, hop1, hop2, w_ref, w_pair, w_acc, w_hop1, w_hop2, halo_out, halo_in, col_tab, row_tab, high, low,
    term, far_out, far_in, near_out, near_in,
    pair_sem, hop1_sem, hop2_sem, send_sem, w_sem, halo_sem, far_sem, near_sem, end_sem, small_sem,
):
    taps_copy = pltpu.make_async_copy(det_hbm, det_ref, small_sem.at[0])
    taps_copy.start()
    me = lax.axis_index("patch")
    band = lax.axis_index("band")
    core = lax.rem(me, 2)
    place = (lax.div(me, 2 * SIDE), lax.rem(lax.div(me, 2), SIDE))
    partner = me + 1 - 2 * core
    before = lax.rem(me + NPATCH - 1, NPATCH)
    after = lax.rem(me + 1, NPATCH)
    beside = lax.rem(me + NPATCH - 1 + 2 * core, NPATCH)

    def moved(axis, step):
        there = list(place)
        there[axis] = wrap(place[axis] + step)
        return patch_index(there[0], there[1], core)

    barrier = pltpu.get_barrier_semaphore()
    for device in (partner, beside, moved(0, 1), moved(0, -1), moved(1, 1), moved(1, -1)):
        pl.semaphore_signal(barrier, inc=1, device_id={"patch": device})
    above = lax.rem(band + 1, NBAND)
    below = lax.rem(band + NBAND - 1, NBAND)
    for device in (above, below):
        pl.semaphore_signal(barrier, inc=1, device_id={"band": device})
    pl.semaphore_wait(barrier, 8)

    def remote(src, dst, send, recv, device, axis="patch"):
        return pltpu.make_async_remote_copy(
            src_ref=src, dst_ref=dst, send_sem=send, recv_sem=recv, device_id={axis: device}
        )

    def dest(s, h, k):
        axis, step = STREAMS[s]
        first = wrap(place[axis] - step * (1 + h))
        other = wrap(place[1 - axis] - step * (1 + k))
        return (first, other) if axis == 0 else (other, first)

    def tile(s, h, k, parity):
        y, z = dest(s, h, k)
        return patch_index(y, z, parity) * SLOTS + s

    next1 = [moved(axis, step) for axis, step in STREAMS]
    next2 = [moved(1 - axis, step) for axis, step in STREAMS]

    def send_pair(s, h, k):
        remote(
            d_ref.at[tile(s, h, k, 1 - core)], pair.at[s, h, k], send_sem.at[0], pair_sem.at[s, h, k], partner
        ).start()

    def wait_pair(s, h, k):
        remote(pair.at[s, h, k], pair.at[s, h, k], send_sem.at[0], pair_sem.at[s, h, k], partner).wait_recv()

    def hop1_copy(s, h, k):
        return remote(pair.at[s, h, k], hop1.at[s, h, k], send_sem.at[1], hop1_sem.at[s, h, k], next1[s])

    def hop2_copy(s, k, sub):
        rows = pl.ds(sub * HALF, HALF)
        return remote(
            pair.at[s, 3, k, rows], hop2.at[s, k, rows], send_sem.at[2], hop2_sem.at[s, k, sub], next2[s]
        )

    table = d_ref[NPATCH * SLOTS]
    table = table[:, 0:128].astype(F32) + table[:, 128:256].astype(F32)
    w_ref[...] = table.reshape(2, SIDE, SIDE, 8, 128)
    w_exchange = remote(w_ref.at[1 - core], w_pair, send_sem.at[3], w_sem.at[0], partner)
    w_exchange.start()

    def send_pairs(h, first):
        @pl.loop(first, first + 2)
        def _(k):
            for s in range(SLOTS):
                send_pair(s, h, k)

    send_pairs(0, 0)
    w_exchange.wait_recv()

    def w_here(h):
        z = wrap(place[1] - 1 - h)
        return w_ref[core, z] + w_pair[z]

    def w_copy1(h):
        return remote(w_acc.at[h], w_hop1.at[h], send_sem.at[4 + h], w_sem.at[1 + h], moved(1, 1))

    def w_copy2(k):
        return remote(w_acc.at[3 + k], w_hop2.at[k], send_sem.at[7 + k], w_sem.at[4 + k], moved(0, 1))

    def here(s, h, k, rows=slice(0, BLK)):
        y, z = dest(s, h, k)
        height = rows.stop - rows.start
        wide = lambda row: jnp.broadcast_to(jnp.concatenate([row, row], axis=1), (height, BLK))
        mine = jnp.where(
            wide(w_ref[core, z, y, s : s + 1]) > 0.0, d_ref[tile(s, h, k, core), rows].astype(F32), 0.0
        )
        other = jnp.where(wide(w_pair[z, y, s : s + 1]) > 0.0, pair[s, h, k, rows].astype(F32), 0.0)
        return mine + other

    def start_units(first, *ahead):
        @pl.loop(first, first + 2)
        def _(k):
            for later, start in ahead:
                for s in range(SLOTS):
                    send_pair(s, later, k - first + start)
            for s in range(SLOTS):
                wait_pair(s, 0, k)
                pair[s, 0, k] = here(s, 0, k).astype(BF16)
                hop1_copy(s, 0, k).start()

    def pass_units(h, first, *ahead):
        @pl.loop(first, first + 2)
        def _(k):
            for later, start in ahead:
                for s in range(SLOTS):
                    send_pair(s, later, k - first + start)
            for s in range(SLOTS):
                wait_pair(s, h, k)
                total = here(s, h, k)
                hop1_copy(s, h - 1, k).wait_recv()
                pair[s, h, k] = (total + hop1[s, h - 1, k].astype(F32)).astype(BF16)
                hop1_copy(s, h, k).start()

    def gathered(s, k, sub):
        rows = slice(sub * HALF, (sub + 1) * HALF)
        if sub == 0:
            wait_pair(s, 3, k)
            hop1_copy(s, 2, k).wait_recv()
        total = here(s, 3, k, rows) + hop1[s, 2, k, rows].astype(F32)
        if k > 0:
            hop2_copy(s, k - 1, sub).wait_recv()
            total = total + hop2[s, k - 1, rows].astype(F32)
        return total

    def turn_units(k):
        for sub in range(2):
            for s in range(SLOTS):
                pair[s, 3, k, sub * HALF : (sub + 1) * HALF] = gathered(s, k, sub).astype(BF16)
                hop2_copy(s, k, sub).start()

    def w_step(n):
        if n > 0:
            (w_copy1(n - 1) if n < 4 else w_copy2(n - 4)).wait_recv()
        if n < 3:
            w_acc[n] = w_here(n) + w_hop1[n - 1] if n > 0 else w_here(n)
            w_copy1(n).start()
        else:
            w_acc[n] = w_here(3) + w_hop1[2] if n == 3 else w_acc[3] + w_hop2[n - 4]
            w_copy2(n - 3).start()

    w_step(0)
    start_units(0, (1, 0))
    taps_copy.wait()
    build_tables(det_ref, col_tab, row_tab)
    pass_units(1, 0, (2, 0))
    w_step(1)
    pass_units(2, 0, (0, 2))
    w_step(2)
    start_units(2, (3, 0), (1, 2))
    w_step(3)
    turn_units(0)
    pass_units(1, 2, (2, 2))
    w_step(4)
    turn_units(1)
    pass_units(2, 2, (3, 2))
    w_step(5)
    turn_units(2)
    w_copy2(2).wait_recv()
    weight_sum = w_acc[3, place[0]] + w_hop2[2, place[0]]
    scale = 1.0 / jnp.maximum(weight_sum, 1.0)

    def halo_copy(d, sub):
        device = after if d == 0 else before
        return remote(
            halo_out.at[d, sub], halo_in.at[d, sub], end_sem.at[2 * sub + d], halo_sem.at[2 * sub + d], device
        )

    lane = lax.broadcasted_iota(jnp.int32, (EDGE, 128), 1) - lax.broadcasted_iota(jnp.int32, (EDGE, 128), 0)
    pick = [jnp.where(lane == first, 1.0, 0.0).astype(BF16) for first in (128 - EDGE, 0)]

    for sub in range(2):
        for s in range(SLOTS):
            value = gathered(s, 3, sub) * jnp.broadcast_to(scale[s : s + 1, 0:1], (HALF, BLK))
            top = (s // 2) * BLK + sub * HALF
            rows = slice(top, top + HALF)
            cols = slice((s % 2) * BLK, (s % 2 + 1) * BLK)
            img_ref[rows, cols] = value
            high[rows, cols], low[rows, cols] = split(value)
        tops = [half * BLK + sub * HALF for half in range(2)]
        for d, lane in enumerate((PH - 128, 0)):
            slab = jnp.concatenate([high[top : top + HALF, lane : lane + 128] for top in tops], axis=0)
            outermost = lax.dot_general(pick[d], slab, (((1,), (1,)), ((), ())), preferred_element_type=F32)
            halo_out[d, sub] = outermost.astype(BF16)
        for d in range(2):
            halo_copy(d, sub).start()

    high[...], low[...] = split(dot3(high[...], low[...], col_tab[0], col_tab[1]))
    height = PH // NBAND
    part = height // 2
    opposite = lax.rem(band + 2, NBAND)
    near = (above, below)
    over_noise = 1.0 / noise_ref[...]

    def row_tables(chunks):
        return [jnp.concatenate([row_tab[n, g] for g in chunks], axis=0) for n in range(2)]

    def rows_of(first, chunks, main=None):
        tables = row_tables(chunks)
        row = dot3(*tables, high[...], low[...]) if main is None else main
        edge = dot3(*tables, edge_high, edge_low)
        on_left = lax.broadcasted_iota(jnp.int32, edge.shape, 1) < 64
        row = jnp.concatenate(
            [
                row[:, 0:128] + jnp.where(on_left, edge, 0.0),
                row[:, 128 : PH - 128],
                row[:, PH - 128 : PH] + jnp.where(on_left, 0.0, edge),
            ],
            axis=1,
        )
        squares = row * row * jnp.broadcast_to(over_noise, row.shape)
        for n in range(len(chunks)):
            term[first + n] = squares[n * height : (n + 1) * height]

    far_copy = lambda d: remote(far_out.at[d], far_in.at[d], end_sem.at[4 + d], far_sem.at[d], near[d], "band")
    near_copy = lambda d, n: remote(
        near_out.at[d, n], near_in.at[d, n], end_sem.at[6 + 2 * d + n], near_sem.at[2 * d + n], near[d], "band"
    )

    def send_early(d):
        near_out[d, 1 - d] = term[1 + d, (1 - d) * part : (2 - d) * part].astype(BF16)
        near_copy(d, 1 - d).start()

    main = dot3(*row_tables((opposite,)), high[...], low[...])
    for sub in range(2):
        for d in range(2):
            halo_copy(d, sub).wait_recv()
    dot = lambda a, b: jnp.dot(a, b, preferred_element_type=F32)
    sides = [
        jnp.concatenate([halo_in[d, n % 2, :, n // 2 * HALF : n // 2 * HALF + HALF] for n in range(4)], axis=1)
        for d in range(2)
    ]
    gap = jnp.zeros((128 - EDGE, PH), BF16)
    sides = jnp.concatenate([gap, *sides, gap], axis=0)
    edge_turned = jnp.zeros((128, PH), F32)
    for n in range(2):
        corners = jnp.concatenate([row_tab[n, 1, :, 0:128], row_tab[n, 0, :, 128:256]], axis=1)
        edge_turned = edge_turned + jnp.dot(corners, sides, preferred_element_type=F32)
    edge_high, edge_low = split(edge_turned.T)
    rows_of(0, (opposite,), main)
    for d in range(2):
        far_out[d] = term[0, d * part : (d + 1) * part].astype(BF16)
        far_copy(d).start()
    rows_of(1, (above, below))
    send_early(0)
    send_early(1)
    rows_of(3, (band,))
    for d in range(2):
        far_copy(d).wait_recv()
        near_out[d, d] = (term[1 + d, d * part : (d + 1) * part] + far_in[d].astype(F32)).astype(BF16)
        near_copy(d, d).start()
    for n in range(2):
        near_copy(0, n).wait_recv()
        near_copy(1, n).wait_recv()
        own = term[3, n * part : (n + 1) * part]
        chi_ref[n * part : (n + 1) * part] = own + (near_in[0, n].astype(F32) + near_in[1, n].astype(F32))

    for index, ref in enumerate((pair, hop1, hop2)):
        remote(ref, ref, send_sem.at[index], w_sem.at[0], partner).wait_send()
    w_exchange.wait_send()
    for h in range(SIDE - 1):
        w_copy1(h).wait_send()
        w_copy2(h).wait_send()
    for sub in range(2):
        for d in range(2):
            halo_copy(d, sub).wait_send()
    for d in range(2):
        far_copy(d).wait_send()
        for n in range(2):
            near_copy(d, n).wait_send()


def reduce_partials(partial, det_taps, noise_var):
    hbm = pl.BlockSpec(memory_space=pltpu.HBM)
    keep = lambda x: pltpu.with_memory_space_constraint(x, pltpu.HBM)
    vmem = pl.BlockSpec(memory_space=pltpu.VMEM)
    dma = pltpu.SemaphoreType.DMA
    height = PH // NBAND
    return pl.pallas_call(
        reduce_kernel,
        out_shape=(
            jax.ShapeDtypeStruct((PH, PH), F32),
            jax.ShapeDtypeStruct((height, PH), F32),
        ),
        in_specs=[vmem, hbm, vmem],
        out_specs=(vmem, vmem),
        scratch_shapes=[
            pltpu.SMEM(det_taps.shape, F32),
            pltpu.VMEM((SLOTS, SIDE, SIDE, BLK, BLK), BF16),
            pltpu.VMEM((SLOTS, SIDE - 1, SIDE, BLK, BLK), BF16),
            pltpu.VMEM((SLOTS, SIDE - 1, BLK, BLK), BF16),
            pltpu.VMEM((2, SIDE, SIDE, 8, 128), F32),
            pltpu.VMEM((SIDE, SIDE, 8, 128), F32),
            pltpu.VMEM((2 * SIDE - 2, SIDE, 8, 128), F32),
            pltpu.VMEM((SIDE - 1, SIDE, 8, 128), F32),
            pltpu.VMEM((SIDE - 1, SIDE, 8, 128), F32),
            pltpu.VMEM((2, 2, EDGE, BLK), BF16),
            pltpu.VMEM((2, 2, EDGE, BLK), BF16),
            pltpu.VMEM((2, PH, PH), BF16),
            pltpu.VMEM((2, PH // 128, 128, PH), BF16),
            pltpu.VMEM((PH, PH), BF16),
            pltpu.VMEM((PH, PH), BF16),
            pltpu.VMEM((NBAND, height, PH), F32),
            pltpu.VMEM((2, height // 2, PH), BF16),
            pltpu.VMEM((2, height // 2, PH), BF16),
            pltpu.VMEM((2, 2, height // 2, PH), BF16),
            pltpu.VMEM((2, 2, height // 2, PH), BF16),
            dma((SLOTS, SIDE, SIDE)),
            dma((SLOTS, SIDE - 1, SIDE)),
            dma((SLOTS, SIDE - 1, 2)),
            dma((10,)),
            dma((7,)),
            dma((4,)),
            dma((2,)),
            dma((4,)),
            dma((10,)),
            dma((1,)),
        ],
        compiler_params=pltpu.CompilerParams(
            vmem_limit_bytes=36 << 20, collective_id=0, has_side_effects=True
        ),
        name="reduce_partials",
    )(partial, keep(det_taps), noise_var)


def write_kernel(image, chi, image_hbm, chi_hbm, sems):
    parts = [pl.ds(n * HALF, HALF) for n in range(PH // HALF)]
    copies = [pltpu.make_async_copy(image.at[rows], image_hbm.at[rows], sems.at[n]) for n, rows in enumerate(parts)]
    copies.append(pltpu.make_async_copy(chi, chi_hbm, sems.at[len(parts)]))
    for copy in copies:
        copy.start()
    for copy in copies:
        copy.wait()


def write_out(image, chi):
    hbm = pl.BlockSpec(memory_space=pltpu.HBM)
    vmem = pl.BlockSpec(memory_space=pltpu.VMEM)
    return pl.pallas_call(
        write_kernel,
        out_shape=tuple(jax.ShapeDtypeStruct(x.shape, x.dtype) for x in (image, chi)),
        in_specs=[vmem, vmem],
        out_specs=(hbm, hbm),
        scratch_shapes=[pltpu.SemaphoreType.DMA((PH // HALF + 1,))],
        name="write_out",
    )(*(pltpu.with_memory_space_constraint(x, pltpu.VMEM) for x in (image, chi)))


def local(blocks, dest_patch, dest_slot, weights, psf_taps, det_taps, noise_var):
    partial = match_partials(blocks, dest_patch, dest_slot, weights, psf_taps)
    partial = pltpu.with_memory_space_constraint(partial, pltpu.VMEM)
    image, chi = reduce_partials(partial, det_taps, noise_var.reshape(1, 1))
    image, chi = write_out(image, chi)
    return image[None], chi


def solution(mesh):
    in_specs = (
        P("band", "patch", None, None),
        P("band", "patch"),
        P("band", "patch"),
        P("band", "patch"),
        P("band", "patch", None, None),
        P("band", None),
        P("band"),
    )
    out_specs = (P("band", None, "patch"), P("band", "patch"))
    return jax.shard_map(local, mesh=mesh, in_specs=in_specs, out_specs=out_specs, check_vma=False)
```
